32 devices in a mesh: row: 8 (over z, x), col: 4 (over y, core).
Axes of the slice: x: 2, y: 2, z: 4, core: 2. Of those that a mesh axis runs over, the one named last changes fastest.
Arguments:
- replica_weights: float32 [8, 4, 128, 2048], P('row', 'col'), may hold values from -4.5 to 4.5
- replica_first: float32 [8, 4, 128, 2048], P('row', 'col'), may hold values from -3.9 to 3.9
- replica_second: float32 [8, 4, 128, 2048], P('row', 'col'), may hold values from 0.05 to 8
- replica_grads: float32 [8, 4, 128, 2048], P('row', 'col'), may hold values from -9 to 9
Outputs:
- mean_weights: float32 [128, 2048], replicated
- mean_first: float32 [128, 2048], replicated
- mean_second: float32 [128, 2048], replicated
The draws below stay inside these ranges and needn't reach their ends.
All inputs are finite; a program needn't handle non-finite values.
Results may differ from the reference program's by a relative error of at most 0.00002.
Values sent between devices are 32-bit elements; how exact they have to be, the bound alone decides.
A program may use at most 64 MiB of HBM per device.

```python
import jax
import jax.numpy as jnp
from jax import lax

D = 2048
WROWS = 128
N_ROW = 8
N_COL = 4


def signed_field(key, spread, salt):
    base = jax.random.truncated_normal(jax.random.fold_in(key, salt), -3.0, 3.0, (WROWS, D), jnp.float32)
    jitter = jax.random.truncated_normal(jax.random.fold_in(key, salt + 1), -3.0, 3.0, (N_ROW, N_COL, WROWS, D), jnp.float32)
    return base[None, None] + spread * jitter


def draw_replica_weights(key, part):
    return signed_field(key, 0.5, 11)


def draw_replica_first(key, part):
    return signed_field(key, 0.3, 21)


def draw_replica_grads(key, part):
    return 2.0 * signed_field(key, 0.5, 31)


def draw_replica_second(key, part):
    base = jnp.exp(jax.random.uniform(jax.random.fold_in(key, 41), (WROWS, D), jnp.float32, jnp.log(0.1), jnp.log(4.0)))
    factor = jnp.exp(jax.random.uniform(jax.random.fold_in(key, 42), (N_ROW, N_COL, WROWS, D), jnp.float32, jnp.log(0.5), jnp.log(2.0)))
    return base[None, None] * factor


def setup_inputs(seed: int = 0) -> dict:
    key_list = jax.random.split(jax.random.key(seed), 5)
    return {
        "replica_weights": draw_replica_weights(jax.random.fold_in(key_list[4], 71), 0),
        "replica_first": draw_replica_first(jax.random.fold_in(key_list[4], 71), 0),
        "replica_second": draw_replica_second(jax.random.fold_in(key_list[4], 71), 0),
        "replica_grads": draw_replica_grads(jax.random.fold_in(key_list[4], 71), 0),
    }


bias_one = 0.9999734386011124
bias_two = 0.994079470779666

def reference(replica_weights, replica_first, replica_second, replica_grads):
    first = 0.9 * replica_first + 0.1 * replica_grads
    second = 0.95 * replica_second + 0.05 * replica_grads * replica_grads
    update = first / bias_one / (jnp.sqrt(second / bias_two) + 1e-08) + 0.1 * replica_weights
    weights = replica_weights - 0.003 * update
    return (lax.optimization_barrier(jnp.mean(weights, axis=(0, 1))), lax.optimization_barrier(jnp.mean(first, axis=(0, 1))), lax.optimization_barrier(jnp.mean(second, axis=(0, 1))))
```

```python
import functools

import jax
import jax.numpy as jnp
from jax import lax
from jax.experimental import pallas as pl
from jax.experimental.pallas import tpu as pltpu
from jax.sharding import PartitionSpec as P

bias_one = 0.9999734386011124
bias_two = 0.994079470779666
MESH = pl.DeviceIdType.MESH
GROUP = 16


COMPUTE_AT = (0, 19, 25, 12, 4, 1, 3, 2)
PIECES = (
    ("gF", (16, 32, 46, 82, 104, 135, 146)),
    ("A1", (5, 22, 49, 78, 100, 118, 170)),
    ("A2", (6, 50, 75, 96, 115, 138, 152)),
    ("gF", (20, 37, 54, 77, 97, 116, 147)),
    ("A2", (44, 62, 80, 102, 123, 143, 151)),
    ("A2", (47, 70, 88, 114, 139, 162, 173)),
    ("A1", (45, 64, 84, 103, 127, 144, 158)),
    ("A1", (41, 58, 71, 93, 119, 149, 167)),
    ("gF", (31, 55, 68, 87, 121, 155, 166)),
    ("gF", (23, 61, 73, 99, 126, 148, 169)),
    ("A2", (21, 53, 76, 98, 120, 156, 168)),
    ("A2", (27, 74, 95, 112, 132, 154, 172)),
    ("A1", (15, 39, 60, 92, 122, 145, 153)),
    ("gF", (35, 56, 69, 94, 134, 164, 176)),
    ("A1", (24, 42, 65, 85, 109, 141, 142)),
    ("y4", (11, 28, 40, 63, 105, 124, 150, 163)),
    ("gF", (7, 38, 90, 108, 130, 157, 175)),
    ("A2", (18, 36, 59, 81, 106, 128, 129)),
    ("gF", (17, 33, 51, 86, 117, 140, 165)),
    ("A1", (10, 29, 83, 107, 133, 159, 171)),
    ("A2", (13, 30, 57, 72, 101, 125, 137)),
    ("gF", (9, 34, 52, 79, 131, 160, 177)),
    ("x4", (14, 43, 67, 91, 113, 136, 161, 174)),
    ("A1", (8, 26, 48, 66, 89, 110, 111)),
)

def stage_orders(rows, cols):
    row_bits = [("row", b) for b in range((rows - 1).bit_length())]
    col_bits = [("col", b) for b in range((cols - 1).bit_length())]
    core, ys, xs, zs = col_bits[0], col_bits[1:], row_bits[0], row_bits[1:]
    near, far = zs[0], tuple(zs[1:])
    single = lambda bits: [((bit,), False) for bit in bits]
    first = ((core,), False)
    return {
        "x4": [first, ((xs,), False), *single(ys), (tuple(zs), False)],
        "y4": [first, *single(ys), ((xs,), False), (tuple(zs), False)],
        "h": [first, *single(zs), ((xs, *ys), False)],
        "A1": [first, ((xs,), False), ((*ys, near), False), (far, True)],
        "A2": [first, *single(ys), ((xs, near), False), (far, True)],
        "gF": [first, ((near,), False), ((xs, *ys), False), (far, True)],
        "c": [first, ((xs, *ys, near), False), (far, True)],
        "d": [first, ((xs, *ys), False), (tuple(zs), False)],
        "dA": [first, ((xs, *ys), False), (tuple(zs), True)],
    }


def flips(stage, m):
    return tuple(bit for j, bit in enumerate(stage[0]) if m >> j & 1)


def rounds(order):
    return 2 * len(order) - (1 if order[-1][1] else 0)


def plan(tiles, orders, devices):
    pieces, keyed = [], []
    for i, first in enumerate(range(0, tiles, devices)):
        at = COMPUTE_AT[i % len(COMPUTE_AT)]
        keyed.append((at, -1, "compute", first))
        for array in range(3):
            name, keys = PIECES[len(pieces) % len(PIECES)]
            for k in range(rounds(orders[name])):
                extra = max(0, k + 1 - len(keys))
                at = max(at, keys[min(k, len(keys) - 1)] + extra)
                keyed.append((at, len(pieces), k, len(pieces)))
            at = COMPUTE_AT[i % len(COMPUTE_AT)]
            pieces.append((array, first, devices, name))
    keyed.sort(key=lambda entry: entry[:2] + (0 if entry[2] == "compute" else entry[2],))
    events = [("compute", at) if k == "compute" else (at, k) for _, _, k, at in keyed]
    return pieces, events


def for_groups(count, body):
    if count <= GROUP:
        body(0, count)
    else:
        def step(i, carry):
            body(i * GROUP, GROUP)
            return carry

        lax.fori_loop(0, count // GROUP, step, 0)


def kernel(rows, cols, orders, pieces, events, w_hbm, f_hbm, s_hbm, g_hbm, ow, of, os, ins, acc, got, wide, in_sem, send_sem, recv_sem):
    me = {"row": lax.axis_index("row"), "col": lax.axis_index("col")}
    outs = (ow, of, os)
    every_bit = sorted({bit for stage in orders["x4"] for bit in stage[0]})
    value = {bit: lax.rem(me[bit[0]] // (2 ** bit[1]), 2) for bit in every_bit}

    def peer(bits):
        other = dict(me)
        for bit in bits:
            other[bit[0]] = other[bit[0]] + (1 - 2 * value[bit]) * (2 ** bit[1])
        return other["row"], other["col"]

    spans = sorted({(first, count) for _, first, count, _ in pieces})
    counts = dict(spans)
    loads = {}
    for i, (first, count) in enumerate(spans):
        for k, src in enumerate((w_hbm, f_hbm, s_hbm, g_hbm)):
            loads[first, k] = pltpu.make_async_copy(
                src.at[pl.ds(first, count)], ins.at[k, pl.ds(first, count)], in_sem.at[k, i]
            )
            loads[first, k].start()

    used = {piece[3] for piece in pieces}
    met = sorted({flips(st, m) for o in used for st in orders[o] for m in range(1, 1 << len(st[0]))})
    barrier = pltpu.get_barrier_semaphore()
    for bits in met:
        pl.semaphore_signal(barrier, inc=1, device_id=peer(bits), device_id_type=MESH)
    entered = []

    part, size, slot = {}, {}, {}
    slots = 0
    for p, (array, first, count, order) in enumerate(pieces):
        off, n = first, count
        for s, (bits, full) in enumerate(orders[order]):
            n = n if full else n >> len(bits)
            size[p, s] = n
            for m in range(1 << len(bits)):
                at = off
                for j, bit in enumerate(() if full else bits):
                    v = value[bit]
                    at = at + (1 - v if m >> j & 1 else v) * (n << j)
                part[p, s, m] = at
                if m:
                    slot[p, s, m] = slots
                    slots += 2
            off = part[p, s, 0]

    def reduce_copy(p, s, m):
        array, n = pieces[p][0], size[p, s]
        land = wide.at[m - 1] if orders[pieces[p][3]][s][1] else got
        return pltpu.make_async_remote_copy(
            src_ref=acc.at[array, pl.ds(part[p, s, m], n)],
            dst_ref=land.at[array, pl.ds(part[p, s, 0], n)],
            send_sem=send_sem.at[slot[p, s, m]],
            recv_sem=recv_sem.at[slot[p, s, m]],
            device_id=peer(flips(orders[pieces[p][3]][s], m)),
            device_id_type=MESH,
        )

    def gather_copy(p, s, m):
        here = outs[pieces[p][0]].at[pl.ds(part[p, s, 0], size[p, s])]
        return pltpu.make_async_remote_copy(
            src_ref=here,
            dst_ref=here,
            send_sem=send_sem.at[slot[p, s, m] + 1],
            recv_sem=recv_sem.at[slot[p, s, m] + 1],
            device_id=peer(flips(orders[pieces[p][3]][s], m)),
            device_id_type=MESH,
        )

    def others(p, s):
        return range(1, 1 << len(orders[pieces[p][3]][s][0]))

    copies = []

    def go(copy):
        copy.start()
        copies.append(copy)

    def total(p, s, at, n):
        array = pieces[p][0]
        shift = at - part[p, s, 0]
        value = acc[array, pl.ds(at, n)]
        for m in others(p, s):
            land = wide.at[m - 1] if orders[pieces[p][3]][s][1] else got
            value = value + land[array, pl.ds(part[p, s, m] + shift, n)]
        return value

    def add(p, s, at, n):
        def body(i, m):
            acc[pieces[p][0], pl.ds(at + i, m)] = total(p, s, at + i, m)

        for_groups(n, body)

    def adamw(first, count):
        def body(i, m):
            here = pl.ds(first + i, m)
            old, grad = ins[0, here], ins[3, here]
            new_first = 0.9 * ins[1, here] + 0.1 * grad
            new_second = 0.95 * ins[2, here] + 0.05 * grad * grad
            update = (new_first * (1.0 / bias_one)) / (
                jnp.sqrt(new_second * (1.0 / bias_two)) + 1e-08
            ) + 0.1 * old
            acc[0, here] = old - 0.003 * update
            acc[1, here] = new_first
            acc[2, here] = new_second

        for_groups(count, body)

    scale = 1.0 / (rows * cols)
    for p, k in events:
        if p == "compute":
            for j in range(4):
                loads[k, j].wait()
            adamw(k, counts[k])
            if not entered:
                pl.semaphore_wait(barrier, len(met))
                entered.append(True)
            for q, piece in enumerate(pieces):
                if piece[1] == k:
                    for m in others(q, 0):
                        go(reduce_copy(q, 0, m))
            continue
        order = orders[pieces[p][3]]
        steps, full = len(order), order[-1][1]
        s = k if k < steps else 2 * steps - 1 - full - k
        for m in others(p, s):
            (reduce_copy if k < steps else gather_copy)(p, s, m).wait_recv()
        if k + 1 < steps:
            n = size[p, s + 1]
            if not order[s + 1][1]:
                for m in others(p, s + 1):
                    add(p, s, part[p, s + 1, m], n)
                    go(reduce_copy(p, s + 1, m))
                add(p, s, part[p, s + 1, 0], n)
            else:
                add(p, s, part[p, s + 1, 0], n)
                for m in others(p, s + 1):
                    go(reduce_copy(p, s + 1, m))
        else:
            if k + 1 == steps:
                at, n = part[p, s, 0], size[p, s]
                outs[pieces[p][0]][pl.ds(at, n)] = total(p, s, at, n) * scale
            s = 2 * steps - 2 - full - k
            if s >= 0:
                for m in others(p, s):
                    go(gather_copy(p, s, m))
    for copy in copies:
        copy.wait_send()


def store(a, b, c, out_a, out_b, out_c, sem):
    copies = [
        pltpu.make_async_copy(src, dst, sem.at[i])
        for i, (src, dst) in enumerate(((a, out_a), (b, out_b), (c, out_c)))
    ]
    for copy in copies:
        copy.start()
    for copy in copies:
        copy.wait()


def as_tiles(x):
    r, c = x.shape
    return x.reshape(r // 8, 8, c // 128, 128).transpose(0, 2, 1, 3).reshape(r * c // 1024, 8, 128)


def from_tiles(x, shape):
    r, c = shape
    return x.reshape(r // 8, c // 128, 8, 128).transpose(0, 2, 1, 3).reshape(r, c)


def solution(mesh):
    rows, cols = mesh.shape["row"], mesh.shape["col"]

    def on_device(*arrays):
        shape = arrays[0].shape[2:]
        tiles = shape[0] * shape[1] // 1024
        orders = stage_orders(rows, cols)
        pieces, events = plan(tiles, orders, rows * cols)
        slots = sum(2 * ((1 << len(st[0])) - 1) for piece in pieces for st in orders[piece[3]])
        most = max([len(st[0]) for piece in pieces for st in orders[piece[3]] if st[1]], default=1)
        spans = len({piece[1] for piece in pieces})
        result = pl.pallas_call(
            functools.partial(kernel, rows, cols, orders, pieces, events),
            out_shape=(pltpu.VMEM((tiles, 8, 128), jnp.float32),) * 3,
            in_specs=[pl.BlockSpec(memory_space=pltpu.HBM)] * 4,
            out_specs=(pl.BlockSpec(memory_space=pltpu.VMEM),) * 3,
            scratch_shapes=[
                pltpu.VMEM((4, tiles, 8, 128), jnp.float32),
                pltpu.VMEM((3, tiles, 8, 128), jnp.float32),
                pltpu.VMEM((3, tiles, 8, 128), jnp.float32),
                pltpu.VMEM(((1 << most) - 1, 3, tiles, 8, 128), jnp.float32),
                pltpu.SemaphoreType.DMA((4, spans)),
                pltpu.SemaphoreType.DMA((slots,)),
                pltpu.SemaphoreType.DMA((slots,)),
            ],
            compiler_params=pltpu.CompilerParams(
                collective_id=0, has_side_effects=True, vmem_limit_bytes=48 * 1024 * 1024
            ),
        )(*(pltpu.with_memory_space_constraint(as_tiles(x[0, 0]), pltpu.HBM) for x in arrays))
        result = pl.pallas_call(
            store,
            out_shape=(jax.ShapeDtypeStruct((tiles, 8, 128), jnp.float32),) * 3,
            in_specs=[pl.BlockSpec(memory_space=pltpu.VMEM)] * 3,
            out_specs=(pl.BlockSpec(memory_space=pltpu.HBM),) * 3,
            scratch_shapes=[pltpu.SemaphoreType.DMA((3,))],
        )(*(pltpu.with_memory_space_constraint(x, pltpu.VMEM) for x in result))
        return tuple(from_tiles(x, shape) for x in result)

    in_specs = (P("row", "col", None, None),) * 4
    return jax.shard_map(
        on_device, mesh=mesh, in_specs=in_specs, out_specs=(P(), P(), P()), check_vma=False
    )
```

```python
import functools

import jax
import jax.numpy as jnp
from jax import lax
from jax.experimental import pallas as pl
from jax.experimental.pallas import tpu as pltpu
from jax.sharding import PartitionSpec as P

bias_one = 0.9999734386011124
bias_two = 0.994079470779666
MESH = pl.DeviceIdType.MESH
GROUP = 16


COMPUTE_AT = (0, 19, 25, 12, 4, 1, 3, 2)
PIECES = (
    ("gF", (16, 32, 46, 82, 104, 135, 146)),
    ("A1", (5, 22, 49, 78, 100, 118, 170)),
    ("A2", (6, 50, 75, 96, 115, 138, 152)),
    ("gF", (20, 37, 54, 77, 97, 116, 147)),
    ("A2", (44, 62, 80, 102, 123, 143, 151)),
    ("A2", (47, 70, 88, 114, 139, 162, 173)),
    ("A1", (45, 64, 84, 103, 127, 144, 158)),
    ("A1", (41, 58, 71, 93, 119, 149, 167)),
    ("gF", (31, 55, 68, 87, 121, 155, 166)),
    ("gF", (23, 61, 73, 99, 126, 148, 169)),
    ("A2", (21, 53, 76, 98, 120, 156, 168)),
    ("A2", (27, 74, 95, 112, 132, 154, 172)),
    ("A1", (15, 39, 60, 92, 122, 145, 153)),
    ("gF", (35, 56, 69, 94, 134, 164, 176)),
    ("A1", (24, 42, 65, 85, 109, 141, 142)),
    ("y4", (11, 28, 40, 63, 105, 124, 150, 163)),
    ("gF", (7, 38, 90, 108, 130, 157, 175)),
    ("A2", (18, 36, 59, 81, 106, 128, 129)),
    ("gF", (17, 33, 51, 86, 117, 140, 165)),
    ("A1", (10, 29, 83, 107, 133, 159, 171)),
    ("A2", (13, 30, 57, 72, 101, 125, 137)),
    ("gF", (9, 34, 52, 79, 131, 160, 177)),
    ("x4", (14, 43, 67, 91, 113, 136, 161, 174)),
    ("A1", (8, 26, 48, 66, 89, 110, 111)),
)

def stage_orders(rows, cols):
    row_bits = [("row", b) for b in range((rows - 1).bit_length())]
    col_bits = [("col", b) for b in range((cols - 1).bit_length())]
    core, ys, xs, zs = col_bits[0], col_bits[1:], row_bits[0], row_bits[1:]
    near, far = zs[0], tuple(zs[1:])
    single = lambda bits: [((bit,), False) for bit in bits]
    first = ((core,), False)
    return {
        "x4": [first, ((xs,), False), *single(ys), (tuple(zs), False)],
        "y4": [first, *single(ys), ((xs,), False), (tuple(zs), False)],
        "h": [first, *single(zs), ((xs, *ys), False)],
        "A1": [first, ((xs,), False), ((*ys, near), False), (far, True)],
        "A2": [first, *single(ys), ((xs, near), False), (far, True)],
        "gF": [first, ((near,), False), ((xs, *ys), False), (far, True)],
        "c": [first, ((xs, *ys, near), False), (far, True)],
        "d": [first, ((xs, *ys), False), (tuple(zs), False)],
        "dA": [first, ((xs, *ys), False), (tuple(zs), True)],
    }


def flips(stage, m):
    return tuple(bit for j, bit in enumerate(stage[0]) if m >> j & 1)


def rounds(order):
    return 2 * len(order) - (1 if order[-1][1] else 0)


def plan(tiles, orders, devices):
    pieces, keyed = [], []
    for i, first in enumerate(range(0, tiles, devices)):
        at = COMPUTE_AT[i % len(COMPUTE_AT)]
        keyed.append((at, -1, "compute", first))
        for array in range(3):
            name, keys = PIECES[len(pieces) % len(PIECES)]
            for k in range(rounds(orders[name])):
                extra = max(0, k + 1 - len(keys))
                at = max(at, keys[min(k, len(keys) - 1)] + extra)
                keyed.append((at, len(pieces), k, len(pieces)))
            at = COMPUTE_AT[i % len(COMPUTE_AT)]
            pieces.append((array, first, devices, name))
    keyed.sort(key=lambda entry: entry[:2] + (0 if entry[2] == "compute" else entry[2],))
    events = [("compute", at) if k == "compute" else (at, k) for _, _, k, at in keyed]
    return pieces, events


def for_groups(count, body):
    if count <= GROUP:
        body(0, count)
    else:
        def step(i, carry):
            body(i * GROUP, GROUP)
            return carry

        lax.fori_loop(0, count // GROUP, step, 0)


def kernel(rows, cols, orders, pieces, events, w_hbm, f_hbm, s_hbm, g_hbm, ow, of, os, ins, acc, got, wide, sent, in_sem, send_sem, recv_sem):
    me = {"row": lax.axis_index("row"), "col": lax.axis_index("col")}
    outs = (ow, of, os)
    every_bit = sorted({bit for stage in orders["x4"] for bit in stage[0]})
    value = {bit: lax.rem(me[bit[0]] // (2 ** bit[1]), 2) for bit in every_bit}

    def peer(bits):
        other = dict(me)
        for bit in bits:
            other[bit[0]] = other[bit[0]] + (1 - 2 * value[bit]) * (2 ** bit[1])
        return other["row"], other["col"]

    spans = sorted({(first, count) for _, first, count, _ in pieces})
    counts = dict(spans)
    loaded = {}
    for i, (first, count) in enumerate(spans):
        for k, src in enumerate((w_hbm, f_hbm, s_hbm, g_hbm)):
            pltpu.make_async_copy(
                src.at[pl.ds(first, count)], ins.at[k, pl.ds(first, count)], in_sem.at[i]
            ).start()
        here = ins.at[:, pl.ds(first, count)]
        loaded[first] = pltpu.make_async_copy(here, here, in_sem.at[i])

    used = {piece[3] for piece in pieces}
    met = sorted({flips(st, m) for o in used for st in orders[o] for m in range(1, 1 << len(st[0]))})
    barrier = pltpu.get_barrier_semaphore()
    for bits in met:
        pl.semaphore_signal(barrier, inc=1, device_id=peer(bits), device_id_type=MESH)
    entered = []

    part, size, slot = {}, {}, {}
    slots = 0
    for p, (array, first, count, order) in enumerate(pieces):
        off, n = first, count
        for s, (bits, full) in enumerate(orders[order]):
            n = n if full else n >> len(bits)
            size[p, s] = n
            for m in range(1 << len(bits)):
                at = off
                for j, bit in enumerate(() if full else bits):
                    v = value[bit]
                    at = at + (1 - v if m >> j & 1 else v) * (n << j)
                part[p, s, m] = at
            off = part[p, s, 0]
            slot[p, s] = slots
            slots += 1 if full else 2

    def reduce_copy(p, s, m):
        array, n = pieces[p][0], size[p, s]
        land = wide.at[m - 1] if orders[pieces[p][3]][s][1] else got
        return pltpu.make_async_remote_copy(
            src_ref=acc.at[array, pl.ds(part[p, s, m], n)],
            dst_ref=land.at[array, pl.ds(part[p, s, 0], n)],
            send_sem=send_sem.at[0],
            recv_sem=recv_sem.at[slot[p, s]],
            device_id=peer(flips(orders[pieces[p][3]][s], m)),
            device_id_type=MESH,
        )

    def gather_copy(p, s, m):
        here = outs[pieces[p][0]].at[pl.ds(part[p, s, 0], size[p, s])]
        return pltpu.make_async_remote_copy(
            src_ref=here,
            dst_ref=here,
            send_sem=send_sem.at[0],
            recv_sem=recv_sem.at[slot[p, s] + 1],
            device_id=peer(flips(orders[pieces[p][3]][s], m)),
            device_id_type=MESH,
        )

    def others(p, s):
        return range(1, 1 << len(orders[pieces[p][3]][s][0]))

    def arrive(p, s, gather):
        array, first = pieces[p][:2]
        here = got.at[array, pl.ds(first, len(others(p, s)) * size[p, s])]
        pltpu.make_async_copy(here, here, recv_sem.at[slot[p, s] + gather]).wait()

    def total(p, s, at, n):
        array = pieces[p][0]
        shift = at - part[p, s, 0]
        value = acc[array, pl.ds(at, n)]
        for m in others(p, s):
            land = wide.at[m - 1] if orders[pieces[p][3]][s][1] else got
            value = value + land[array, pl.ds(part[p, s, m] + shift, n)]
        return value

    def add(p, s, at, n):
        def body(i, m):
            acc[pieces[p][0], pl.ds(at + i, m)] = total(p, s, at + i, m)

        for_groups(n, body)

    def adamw(first, count):
        def body(i, m):
            here = pl.ds(first + i, m)
            old, grad = ins[0, here], ins[3, here]
            new_first = 0.9 * ins[1, here] + 0.1 * grad
            new_second = 0.95 * ins[2, here] + 0.05 * grad * grad
            update = (new_first * (1.0 / bias_one)) / (
                jnp.sqrt(new_second * (1.0 / bias_two)) + 1e-08
            ) + 0.1 * old
            acc[0, here] = old - 0.003 * update
            acc[1, here] = new_first
            acc[2, here] = new_second

        for_groups(count, body)

    scale = 1.0 / (rows * cols)
    for p, k in events:
        if p == "compute":
            loaded[k].wait()
            adamw(k, counts[k])
            if not entered:
                pl.semaphore_wait(barrier, len(met))
                entered.append(True)
            for q, piece in enumerate(pieces):
                if piece[1] == k:
                    for m in others(q, 0):
                        reduce_copy(q, 0, m).start()
            continue
        order = orders[pieces[p][3]]
        steps, full = len(order), order[-1][1]
        s = k if k < steps else 2 * steps - 1 - full - k
        arrive(p, s, 0 if k < steps else 1)
        if k + 1 < steps:
            n = size[p, s + 1]
            if not order[s + 1][1]:
                for m in others(p, s + 1):
                    add(p, s, part[p, s + 1, m], n)
                    reduce_copy(p, s + 1, m).start()
                add(p, s, part[p, s + 1, 0], n)
            else:
                add(p, s, part[p, s + 1, 0], n)
                for m in others(p, s + 1):
                    reduce_copy(p, s + 1, m).start()
        else:
            if k + 1 == steps:
                at, n = part[p, s, 0], size[p, s]
                outs[pieces[p][0]][pl.ds(at, n)] = total(p, s, at, n) * scale
            s = 2 * steps - 2 - full - k
            if s >= 0:
                for m in others(p, s):
                    gather_copy(p, s, m).start()
    pltpu.make_async_copy(sent, sent, send_sem.at[0]).wait()


def store(a, b, c, out_a, out_b, out_c, sem):
    copies = [
        pltpu.make_async_copy(src, dst, sem.at[i])
        for i, (src, dst) in enumerate(((a, out_a), (b, out_b), (c, out_c)))
    ]
    for copy in copies:
        copy.start()
    for copy in copies:
        copy.wait()


def as_tiles(x):
    r, c = x.shape
    return x.reshape(r // 8, 8, c // 128, 128).transpose(0, 2, 1, 3).reshape(r * c // 1024, 8, 128)


def from_tiles(x, shape):
    r, c = shape
    return x.reshape(r // 8, c // 128, 8, 128).transpose(0, 2, 1, 3).reshape(r, c)


def solution(mesh):
    rows, cols = mesh.shape["row"], mesh.shape["col"]

    def on_device(*arrays):
        shape = arrays[0].shape[2:]
        tiles = shape[0] * shape[1] // 1024
        orders = stage_orders(rows, cols)
        pieces, events = plan(tiles, orders, rows * cols)
        slots, moved = 0, 0
        for _, _, n, name in pieces:
            for bits, full in orders[name]:
                n = n if full else n >> len(bits)
                slots += 1 if full else 2
                moved += (1 if full else 2) * ((1 << len(bits)) - 1) * n
        most = max([len(st[0]) for piece in pieces for st in orders[piece[3]] if st[1]], default=1)
        spans = len({piece[1] for piece in pieces})
        result = pl.pallas_call(
            functools.partial(kernel, rows, cols, orders, pieces, events),
            out_shape=(pltpu.VMEM((tiles, 8, 128), jnp.float32),) * 3,
            in_specs=[pl.BlockSpec(memory_space=pltpu.HBM)] * 4,
            out_specs=(pl.BlockSpec(memory_space=pltpu.VMEM),) * 3,
            scratch_shapes=[
                pltpu.VMEM((4, tiles, 8, 128), jnp.float32),
                pltpu.VMEM((3, tiles, 8, 128), jnp.float32),
                pltpu.VMEM((3, tiles, 8, 128), jnp.float32),
                pltpu.VMEM(((1 << most) - 1, 3, tiles, 8, 128), jnp.float32),
                pltpu.VMEM((moved, 8, 128), jnp.float32),
                pltpu.SemaphoreType.DMA((spans,)),
                pltpu.SemaphoreType.DMA((1,)),
                pltpu.SemaphoreType.DMA((slots,)),
            ],
            compiler_params=pltpu.CompilerParams(
                collective_id=0, has_side_effects=True, vmem_limit_bytes=48 * 1024 * 1024
            ),
        )(*(pltpu.with_memory_space_constraint(as_tiles(x[0, 0]), pltpu.HBM) for x in arrays))
        result = pl.pallas_call(
            store,
            out_shape=(jax.ShapeDtypeStruct((tiles, 8, 128), jnp.float32),) * 3,
            in_specs=[pl.BlockSpec(memory_space=pltpu.VMEM)] * 3,
            out_specs=(pl.BlockSpec(memory_space=pltpu.HBM),) * 3,
            scratch_shapes=[pltpu.SemaphoreType.DMA((3,))],
        )(*(pltpu.with_memory_space_constraint(x, pltpu.VMEM) for x in result))
        return tuple(from_tiles(x, shape) for x in result)

    in_specs = (P("row", "col", None, None),) * 4
    return jax.shard_map(
        on_device, mesh=mesh, in_specs=in_specs, out_specs=(P(), P(), P()), check_vma=False
    )
```

```python
import functools

import jax
import jax.numpy as jnp
from jax import lax
from jax.experimental import pallas as pl
from jax.experimental.pallas import tpu as pltpu
from jax.sharding import PartitionSpec as P

bias_one = 0.9999734386011124
bias_two = 0.994079470779666
MESH = pl.DeviceIdType.MESH
GROUP = 16


COARSE = 1
COMPUTE_AT = (0, 19, 25, 12, 4, 1, 3, 2)
PIECES = (
    ("gF", (16, 32, 46, 82, 104, 135, 146)),
    ("A1", (5, 22, 49, 78, 100, 118, 170)),
    ("A2", (6, 50, 75, 96, 115, 138, 152)),
    ("gF", (20, 37, 54, 77, 97, 116, 147)),
    ("A2", (44, 62, 80, 102, 123, 143, 151)),
    ("A2", (47, 70, 88, 114, 139, 162, 173)),
    ("A1", (45, 64, 84, 103, 127, 144, 158)),
    ("A1", (41, 58, 71, 93, 119, 149, 167)),
    ("gF", (31, 55, 68, 87, 121, 155, 166)),
    ("gF", (23, 61, 73, 99, 126, 148, 169)),
    ("A2", (21, 53, 76, 98, 120, 156, 168)),
    ("A2", (27, 74, 95, 112, 132, 154, 172)),
    ("A1", (15, 39, 60, 92, 122, 145, 153)),
    ("gF", (35, 56, 69, 94, 134, 164, 176)),
    ("A1", (24, 42, 65, 85, 109, 141, 142)),
    ("y4", (11, 28, 40, 63, 105, 124, 150, 163)),
    ("gF", (7, 38, 90, 108, 130, 157, 175)),
    ("A2", (18, 36, 59, 81, 106, 128, 129)),
    ("gF", (17, 33, 51, 86, 117, 140, 165)),
    ("A1", (10, 29, 83, 107, 133, 159, 171)),
    ("A2", (13, 30, 57, 72, 101, 125, 137)),
    ("gF", (9, 34, 52, 79, 131, 160, 177)),
    ("x4", (14, 43, 67, 91, 113, 136, 161, 174)),
    ("A1", (8, 26, 48, 66, 89, 110, 111)),
)

def stage_orders(rows, cols):
    row_bits = [("row", b) for b in range((rows - 1).bit_length())]
    col_bits = [("col", b) for b in range((cols - 1).bit_length())]
    core, ys, xs, zs = col_bits[0], col_bits[1:], row_bits[0], row_bits[1:]
    near, far = zs[0], tuple(zs[1:])
    single = lambda bits: [((bit,), False) for bit in bits]
    first = ((core,), False)
    return {
        "x4": [first, ((xs,), False), *single(ys), (tuple(zs), False)],
        "y4": [first, *single(ys), ((xs,), False), (tuple(zs), False)],
        "h": [first, *single(zs), ((xs, *ys), False)],
        "A1": [first, ((xs,), False), ((*ys, near), False), (far, True)],
        "A2": [first, *single(ys), ((xs, near), False), (far, True)],
        "gF": [first, ((near,), False), ((xs, *ys), False), (far, True)],
        "x1": [first, ((xs,), False), *single(ys), ((near,), False), (far, True)],
        "y1": [first, *single(ys), ((xs,), False), ((near,), False), (far, True)],
        "x2": [first, ((xs,), False), ((near,), False), *single(ys), (far, True)],
        "y2": [first, *single(ys), ((near,), False), ((xs,), False), (far, True)],
        "ux": [first, ((near,), False), ((xs,), False), *single(ys), (far, True)],
        "uy": [first, ((near,), False), *single(ys), ((xs,), False), (far, True)],
        "c": [first, ((xs, *ys, near), False), (far, True)],
        "d": [first, ((xs, *ys), False), (tuple(zs), False)],
        "dA": [first, ((xs, *ys), False), (tuple(zs), True)],
    }


def flips(stage, m):
    return tuple(bit for j, bit in enumerate(stage[0]) if m >> j & 1)


def rounds(order):
    return 2 * len(order) - (1 if order[-1][1] else 0)


def plan(tiles, orders, devices):
    pieces, keyed = [], []
    shared = min(len(order[-1][0]) if order[-1][1] else 0 for order in (orders[name] for name, _ in PIECES))
    count = COARSE * devices >> shared
    for i, first in enumerate(range(0, tiles, count)):
        at = COMPUTE_AT[i % len(COMPUTE_AT)]
        keyed.append((at, -1, "compute", first))
        for array in range(3):
            name, keys = PIECES[len(pieces) % len(PIECES)]
            for k in range(rounds(orders[name])):
                extra = max(0, k + 1 - len(keys))
                at = max(at, keys[min(k, len(keys) - 1)] + extra)
                keyed.append((at, len(pieces), k, len(pieces)))
            at = COMPUTE_AT[i % len(COMPUTE_AT)]
            pieces.append((array, first, count, name))
    keyed.sort(key=lambda entry: entry[:2] + (0 if entry[2] == "compute" else entry[2],))
    events = [("compute", at) if k == "compute" else (at, k) for _, _, k, at in keyed]
    return pieces, events


def receivers(pieces, events, orders):
    at = {event: i for i, event in enumerate(events)}
    exchanges = []
    for p, (_, first, _, name) in enumerate(pieces):
        order = orders[name]
        last = rounds(order)
        for s, stage in enumerate(order):
            met = [flips(stage, m) for m in range(1, 1 << len(stage[0]))]
            sent = at["compute", first] if s == 0 else at[p, s - 1]
            exchanges.append((sent, at[p, s], p, s, 0, met))
            if not stage[1]:
                exchanges.append((at[p, last - 2 - s], at[p, last - 1 - s], p, s, 1, met))
    heard = {}
    for sent, waited, _, _, _, met in exchanges:
        for bits in met:
            row = heard.setdefault(bits, [len(events)] * (len(events) + 1))
            row[sent] = min(row[sent], waited)
    for row in heard.values():
        for i in reversed(range(len(events))):
            row[i] = min(row[i], row[i + 1])
    index, ends = {}, []
    for sent, waited, p, s, gather, met in sorted(exchanges, key=lambda e: e[:5]):
        free = [
            (end, j) for j, end in enumerate(ends) if all(heard[bits][end] <= sent for bits in met)
        ]
        j = max(free)[1] if free else len(ends)
        ends[j:j + 1] = [waited]
        index[p, s, gather] = j
    return index, len(ends)


def for_groups(count, body):
    if count <= GROUP:
        body(0, count)
    else:
        def step(i, carry):
            body(i * GROUP, GROUP)
            return carry

        lax.fori_loop(0, count // GROUP, step, 0)


def kernel(rows, cols, orders, pieces, events, index, w_hbm, f_hbm, s_hbm, g_hbm, ow, of, os, ins, acc, got, wide, sent, in_sem, send_sem, recv_sem):
    me = {"row": lax.axis_index("row"), "col": lax.axis_index("col")}
    outs = (ow, of, os)
    every_bit = sorted({bit for stage in orders["x4"] for bit in stage[0]})
    value = {bit: lax.rem(me[bit[0]] // (2 ** bit[1]), 2) for bit in every_bit}

    def peer(bits):
        other = dict(me)
        for bit in bits:
            other[bit[0]] = other[bit[0]] + (1 - 2 * value[bit]) * (2 ** bit[1])
        return other["row"], other["col"]

    spans = sorted({(first, count) for _, first, count, _ in pieces})
    counts = dict(spans)
    loaded = {}
    for i, (first, count) in enumerate(spans):
        for k, src in enumerate((w_hbm, f_hbm, s_hbm, g_hbm)):
            pltpu.make_async_copy(
                src.at[pl.ds(first, count)], ins.at[k, pl.ds(first, count)], in_sem.at[i]
            ).start()
        here = ins.at[:, pl.ds(first, count)]
        loaded[first] = pltpu.make_async_copy(here, here, in_sem.at[i])

    used = {piece[3] for piece in pieces}
    met = sorted({flips(st, m) for o in used for st in orders[o] for m in range(1, 1 << len(st[0]))})
    barrier = pltpu.get_barrier_semaphore()
    for bits in met:
        pl.semaphore_signal(barrier, inc=1, device_id=peer(bits), device_id_type=MESH)
    entered = []

    part, size = {}, {}
    for p, (array, first, count, order) in enumerate(pieces):
        off, n = first, count
        for s, (bits, full) in enumerate(orders[order]):
            n = n if full else n >> len(bits)
            size[p, s] = n
            for m in range(1 << len(bits)):
                at = off
                for j, bit in enumerate(() if full else bits):
                    v = value[bit]
                    at = at + (1 - v if m >> j & 1 else v) * (n << j)
                part[p, s, m] = at
            off = part[p, s, 0]

    def reduce_copy(p, s, m):
        array, n = pieces[p][0], size[p, s]
        land = wide.at[m - 1] if orders[pieces[p][3]][s][1] else got
        return pltpu.make_async_remote_copy(
            src_ref=acc.at[array, pl.ds(part[p, s, m], n)],
            dst_ref=land.at[array, pl.ds(part[p, s, 0], n)],
            send_sem=send_sem.at[0],
            recv_sem=recv_sem.at[index[p, s, 0]],
            device_id=peer(flips(orders[pieces[p][3]][s], m)),
            device_id_type=MESH,
        )

    def gather_copy(p, s, m):
        here = outs[pieces[p][0]].at[pl.ds(part[p, s, 0], size[p, s])]
        return pltpu.make_async_remote_copy(
            src_ref=here,
            dst_ref=here,
            send_sem=send_sem.at[0],
            recv_sem=recv_sem.at[index[p, s, 1]],
            device_id=peer(flips(orders[pieces[p][3]][s], m)),
            device_id_type=MESH,
        )

    def others(p, s):
        return range(1, 1 << len(orders[pieces[p][3]][s][0]))

    def arrive(p, s, gather):
        array, first = pieces[p][:2]
        here = got.at[array, pl.ds(first, len(others(p, s)) * size[p, s])]
        pltpu.make_async_copy(here, here, recv_sem.at[index[p, s, gather]]).wait()

    def total(p, s, at, n):
        array = pieces[p][0]
        shift = at - part[p, s, 0]
        value = acc[array, pl.ds(at, n)]
        for m in others(p, s):
            land = wide.at[m - 1] if orders[pieces[p][3]][s][1] else got
            value = value + land[array, pl.ds(part[p, s, m] + shift, n)]
        return value

    def add(p, s, at, n):
        def body(i, m):
            acc[pieces[p][0], pl.ds(at + i, m)] = total(p, s, at + i, m)

        for_groups(n, body)

    def adamw(first, count):
        def body(i, m):
            here = pl.ds(first + i, m)
            old, grad = ins[0, here], ins[3, here]
            new_first = 0.9 * ins[1, here] + 0.1 * grad
            new_second = 0.95 * ins[2, here] + 0.05 * grad * grad
            update = (new_first * (1.0 / bias_one)) / (
                jnp.sqrt(new_second * (1.0 / bias_two)) + 1e-08
            ) + 0.1 * old
            acc[0, here] = old - 0.003 * update
            acc[1, here] = new_first
            acc[2, here] = new_second

        for_groups(count, body)

    scale = 1.0 / (rows * cols)
    for p, k in events:
        if p == "compute":
            loaded[k].wait()
            adamw(k, counts[k])
            if not entered:
                pl.semaphore_wait(barrier, len(met))
                entered.append(True)
            for q, piece in enumerate(pieces):
                if piece[1] == k:
                    for m in others(q, 0):
                        reduce_copy(q, 0, m).start()
            continue
        order = orders[pieces[p][3]]
        steps, full = len(order), order[-1][1]
        s = k if k < steps else 2 * steps - 1 - full - k
        arrive(p, s, 0 if k < steps else 1)
        if k + 1 < steps:
            n = size[p, s + 1]
            if not order[s + 1][1]:
                for m in others(p, s + 1):
                    add(p, s, part[p, s + 1, m], n)
                    reduce_copy(p, s + 1, m).start()
                add(p, s, part[p, s + 1, 0], n)
            else:
                add(p, s, part[p, s + 1, 0], n)
                for m in others(p, s + 1):
                    reduce_copy(p, s + 1, m).start()
        else:
            if k + 1 == steps:
                at, n = part[p, s, 0], size[p, s]
                outs[pieces[p][0]][pl.ds(at, n)] = total(p, s, at, n) * scale
            s = 2 * steps - 2 - full - k
            if s >= 0:
                for m in others(p, s):
                    gather_copy(p, s, m).start()
    pltpu.make_async_copy(sent, sent, send_sem.at[0]).wait()


def store(a, b, c, out_a, out_b, out_c, sem):
    copies = [
        pltpu.make_async_copy(src, dst, sem.at[i])
        for i, (src, dst) in enumerate(((a, out_a), (b, out_b), (c, out_c)))
    ]
    for copy in copies:
        copy.start()
    for copy in copies:
        copy.wait()


def as_tiles(x):
    r, c = x.shape
    return x.reshape(r // 8, 8, c // 128, 128).transpose(0, 2, 1, 3).reshape(r * c // 1024, 8, 128)


def from_tiles(x, shape):
    r, c = shape
    return x.reshape(r // 8, c // 128, 8, 128).transpose(0, 2, 1, 3).reshape(r, c)


def solution(mesh):
    rows, cols = mesh.shape["row"], mesh.shape["col"]

    def on_device(*arrays):
        shape = arrays[0].shape[2:]
        tiles = shape[0] * shape[1] // 1024
        orders = stage_orders(rows, cols)
        pieces, events = plan(tiles, orders, rows * cols)
        index, slots = receivers(pieces, events, orders)
        moved = 0
        for _, _, n, name in pieces:
            for bits, full in orders[name]:
                n = n if full else n >> len(bits)
                moved += (1 if full else 2) * ((1 << len(bits)) - 1) * n
        most = max([len(st[0]) for piece in pieces for st in orders[piece[3]] if st[1]], default=1)
        spans = len({piece[1] for piece in pieces})
        result = pl.pallas_call(
            functools.partial(kernel, rows, cols, orders, pieces, events, index),
            out_shape=(pltpu.VMEM((tiles, 8, 128), jnp.float32),) * 3,
            in_specs=[pl.BlockSpec(memory_space=pltpu.HBM)] * 4,
            out_specs=(pl.BlockSpec(memory_space=pltpu.VMEM),) * 3,
            scratch_shapes=[
                pltpu.VMEM((4, tiles, 8, 128), jnp.float32),
                pltpu.VMEM((3, tiles, 8, 128), jnp.float32),
                pltpu.VMEM((3, tiles, 8, 128), jnp.float32),
                pltpu.VMEM(((1 << most) - 1, 3, tiles, 8, 128), jnp.float32),
                pltpu.VMEM((moved, 8, 128), jnp.float32),
                pltpu.SemaphoreType.DMA((spans,)),
                pltpu.SemaphoreType.DMA((1,)),
                pltpu.SemaphoreType.DMA((slots,)),
            ],
            compiler_params=pltpu.CompilerParams(
                collective_id=0, has_side_effects=True, vmem_limit_bytes=48 * 1024 * 1024
            ),
        )(*(pltpu.with_memory_space_constraint(as_tiles(x[0, 0]), pltpu.HBM) for x in arrays))
        result = pl.pallas_call(
            store,
            out_shape=(jax.ShapeDtypeStruct((tiles, 8, 128), jnp.float32),) * 3,
            in_specs=[pl.BlockSpec(memory_space=pltpu.VMEM)] * 3,
            out_specs=(pl.BlockSpec(memory_space=pltpu.HBM),) * 3,
            scratch_shapes=[pltpu.SemaphoreType.DMA((3,))],
        )(*(pltpu.with_memory_space_constraint(x, pltpu.VMEM) for x in result))
        return tuple(from_tiles(x, shape) for x in result)

    in_specs = (P("row", "col", None, None),) * 4
    return jax.shard_map(
        on_device, mesh=mesh, in_specs=in_specs, out_specs=(P(), P(), P()), check_vma=False
    )
```

```python
import functools

import jax
import jax.numpy as jnp
from jax import lax
from jax.experimental import pallas as pl
from jax.experimental.pallas import tpu as pltpu
from jax.sharding import PartitionSpec as P

bias_one = 0.9999734386011124
bias_two = 0.994079470779666
MESH = pl.DeviceIdType.MESH
GROUP = 16


COARSE = 1
COMPUTE_AT = (0, 14, 6, 1, 2, 3, 8, 19)
PIECES = (
    ("y1", (4, 22, 42, 61, 79, 96, 115, 140, 159)),
    ("d", (5, 36, 63, 84, 102, 127)),
    ("A2", (7, 24, 49, 76, 100, 126, 166)),
    ("A2", (46, 64, 82, 103, 130, 145, 172)),
    ("gF", (16, 33, 58, 80, 104, 136, 165)),
    ("d", (15, 34, 54, 77, 111, 112)),
    ("gF", (41, 62, 87, 108, 131, 153, 163)),
    ("gF", (29, 57, 75, 95, 119, 149, 157)),
    ("y4", (23, 50, 66, 92, 113, 134, 148, 160)),
    ("gF", (9, 26, 44, 67, 105, 125, 133)),
    ("gF", (12, 31, 48, 74, 98, 116, 150)),
    ("gF", (35, 60, 88, 109, 138, 155, 169)),
    ("gF", (13, 45, 73, 93, 121, 143, 161)),
    ("A1", (10, 25, 43, 71, 101, 122, 123)),
    ("d", (11, 30, 52, 90, 139, 144)),
    ("A2", (28, 47, 83, 110, 135, 156, 174)),
    ("A1", (38, 59, 78, 99, 120, 146, 168)),
    ("d", (32, 56, 81, 106, 128, 173)),
    ("d", (17, 37, 86, 118, 142, 170)),
    ("uy", (18, 39, 55, 70, 91, 107, 129, 141, 167)),
    ("A1", (27, 68, 94, 114, 137, 154, 164)),
    ("d", (53, 72, 97, 124, 152, 171)),
    ("gF", (20, 40, 65, 85, 117, 151, 158)),
    ("A1", (21, 51, 69, 89, 132, 147, 162)),
)

def stage_orders(rows, cols):
    row_bits = [("row", b) for b in range((rows - 1).bit_length())]
    col_bits = [("col", b) for b in range((cols - 1).bit_length())]
    core, ys, xs, zs = col_bits[0], col_bits[1:], row_bits[0], row_bits[1:]
    near, far = zs[0], tuple(zs[1:])
    single = lambda bits: [((bit,), False) for bit in bits]
    first = ((core,), False)
    return {
        "x4": [first, ((xs,), False), *single(ys), (tuple(zs), False)],
        "y4": [first, *single(ys), ((xs,), False), (tuple(zs), False)],
        "h": [first, *single(zs), ((xs, *ys), False)],
        "A1": [first, ((xs,), False), ((*ys, near), False), (far, True)],
        "A2": [first, *single(ys), ((xs, near), False), (far, True)],
        "gF": [first, ((near,), False), ((xs, *ys), False), (far, True)],
        "x1": [first, ((xs,), False), *single(ys), ((near,), False), (far, True)],
        "y1": [first, *single(ys), ((xs,), False), ((near,), False), (far, True)],
        "x2": [first, ((xs,), False), ((near,), False), *single(ys), (far, True)],
        "y2": [first, *single(ys), ((near,), False), ((xs,), False), (far, True)],
        "ux": [first, ((near,), False), ((xs,), False), *single(ys), (far, True)],
        "uy": [first, ((near,), False), *single(ys), ((xs,), False), (far, True)],
        "c": [first, ((xs, *ys, near), False), (far, True)],
        "d": [first, ((xs, *ys), False), (tuple(zs), False)],
        "dA": [first, ((xs, *ys), False), (tuple(zs), True)],
    }


def flips(stage, m):
    return tuple(bit for j, bit in enumerate(stage[0]) if m >> j & 1)


def rounds(order):
    return 2 * len(order) - (1 if order[-1][1] else 0)


def plan(tiles, orders, devices):
    pieces, keyed = [], []
    shared = min(len(order[-1][0]) if order[-1][1] else 0 for order in (orders[name] for name, _ in PIECES))
    count = COARSE * devices >> shared
    for i, first in enumerate(range(0, tiles, count)):
        at = COMPUTE_AT[i % len(COMPUTE_AT)]
        keyed.append((at, -1, "compute", first))
        for array in range(3):
            name, keys = PIECES[len(pieces) % len(PIECES)]
            for k in range(rounds(orders[name])):
                extra = max(0, k + 1 - len(keys))
                at = max(at, keys[min(k, len(keys) - 1)] + extra)
                keyed.append((at, len(pieces), k, len(pieces)))
            at = COMPUTE_AT[i % len(COMPUTE_AT)]
            pieces.append((array, first, count, name))
    keyed.sort(key=lambda entry: entry[:2] + (0 if entry[2] == "compute" else entry[2],))
    events = [("compute", at) if k == "compute" else (at, k) for _, _, k, at in keyed]
    return pieces, events


def receivers(pieces, events, orders):
    at = {event: i for i, event in enumerate(events)}
    exchanges = []
    for p, (_, first, _, name) in enumerate(pieces):
        order = orders[name]
        last = rounds(order)
        for s, stage in enumerate(order):
            met = [flips(stage, m) for m in range(1, 1 << len(stage[0]))]
            sent = at["compute", first] if s == 0 else at[p, s - 1]
            exchanges.append((sent, at[p, s], p, s, 0, met))
            if not stage[1]:
                exchanges.append((at[p, last - 2 - s], at[p, last - 1 - s], p, s, 1, met))
    heard = {}
    for sent, waited, _, _, _, met in exchanges:
        for bits in met:
            row = heard.setdefault(bits, [len(events)] * (len(events) + 1))
            row[sent] = min(row[sent], waited)
    for row in heard.values():
        for i in reversed(range(len(events))):
            row[i] = min(row[i], row[i + 1])
    index, ends = {}, []
    for sent, waited, p, s, gather, met in sorted(exchanges, key=lambda e: e[:5]):
        free = [
            (end, j) for j, end in enumerate(ends) if all(heard[bits][end] <= sent for bits in met)
        ]
        j = max(free)[1] if free else len(ends)
        ends[j:j + 1] = [waited]
        index[p, s, gather] = j
    return index, len(ends)


def for_groups(count, body):
    if count <= GROUP:
        body(0, count)
    else:
        def step(i, carry):
            body(i * GROUP, GROUP)
            return carry

        lax.fori_loop(0, count // GROUP, step, 0)


def kernel(rows, cols, orders, pieces, events, index, w_hbm, f_hbm, s_hbm, g_hbm, ow, of, os, ins, acc, got, wide, sent, in_sem, send_sem, recv_sem):
    me = {"row": lax.axis_index("row"), "col": lax.axis_index("col")}
    outs = (ow, of, os)
    every_bit = sorted({bit for stage in orders["x4"] for bit in stage[0]})
    value = {bit: lax.rem(me[bit[0]] // (2 ** bit[1]), 2) for bit in every_bit}

    def peer(bits):
        other = dict(me)
        for bit in bits:
            other[bit[0]] = other[bit[0]] + (1 - 2 * value[bit]) * (2 ** bit[1])
        return other["row"], other["col"]

    spans = sorted({(first, count) for _, first, count, _ in pieces})
    counts = dict(spans)
    loaded = {}
    for i, (first, count) in enumerate(spans):
        for k, src in enumerate((w_hbm, f_hbm, s_hbm, g_hbm)):
            pltpu.make_async_copy(
                src.at[pl.ds(first, count)], ins.at[k, pl.ds(first, count)], in_sem.at[i]
            ).start()
        here = ins.at[:, pl.ds(first, count)]
        loaded[first] = pltpu.make_async_copy(here, here, in_sem.at[i])

    used = {piece[3] for piece in pieces}
    met = sorted({flips(st, m) for o in used for st in orders[o] for m in range(1, 1 << len(st[0]))})
    barrier = pltpu.get_barrier_semaphore()
    for bits in met:
        pl.semaphore_signal(barrier, inc=1, device_id=peer(bits), device_id_type=MESH)
    entered = []

    part, size = {}, {}
    for p, (array, first, count, order) in enumerate(pieces):
        off, n = first, count
        for s, (bits, full) in enumerate(orders[order]):
            n = n if full else n >> len(bits)
            size[p, s] = n
            for m in range(1 << len(bits)):
                at = off
                for j, bit in enumerate(() if full else bits):
                    v = value[bit]
                    at = at + (1 - v if m >> j & 1 else v) * (n << j)
                part[p, s, m] = at
            off = part[p, s, 0]

    def reduce_copy(p, s, m):
        array, n = pieces[p][0], size[p, s]
        land = wide.at[m - 1] if orders[pieces[p][3]][s][1] else got
        return pltpu.make_async_remote_copy(
            src_ref=acc.at[array, pl.ds(part[p, s, m], n)],
            dst_ref=land.at[array, pl.ds(part[p, s, 0], n)],
            send_sem=send_sem.at[0],
            recv_sem=recv_sem.at[index[p, s, 0]],
            device_id=peer(flips(orders[pieces[p][3]][s], m)),
            device_id_type=MESH,
        )

    def gather_copy(p, s, m):
        here = outs[pieces[p][0]].at[pl.ds(part[p, s, 0], size[p, s])]
        return pltpu.make_async_remote_copy(
            src_ref=here,
            dst_ref=here,
            send_sem=send_sem.at[0],
            recv_sem=recv_sem.at[index[p, s, 1]],
            device_id=peer(flips(orders[pieces[p][3]][s], m)),
            device_id_type=MESH,
        )

    def others(p, s):
        return range(1, 1 << len(orders[pieces[p][3]][s][0]))

    def arrive(p, s, gather):
        array, first = pieces[p][:2]
        here = got.at[array, pl.ds(first, len(others(p, s)) * size[p, s])]
        pltpu.make_async_copy(here, here, recv_sem.at[index[p, s, gather]]).wait()

    def total(p, s, at, n):
        array = pieces[p][0]
        shift = at - part[p, s, 0]
        value = acc[array, pl.ds(at, n)]
        for m in others(p, s):
            land = wide.at[m - 1] if orders[pieces[p][3]][s][1] else got
            value = value + land[array, pl.ds(part[p, s, m] + shift, n)]
        return value

    def add(p, s, at, n):
        def body(i, m):
            acc[pieces[p][0], pl.ds(at + i, m)] = total(p, s, at + i, m)

        for_groups(n, body)

    def adamw(first, count):
        def body(i, m):
            here = pl.ds(first + i, m)
            old, grad = ins[0, here], ins[3, here]
            new_first = 0.9 * ins[1, here] + 0.1 * grad
            new_second = 0.95 * ins[2, here] + 0.05 * grad * grad
            update = (new_first * (1.0 / bias_one)) / (
                jnp.sqrt(new_second * (1.0 / bias_two)) + 1e-08
            ) + 0.1 * old
            acc[0, here] = old - 0.003 * update
            acc[1, here] = new_first
            acc[2, here] = new_second

        for_groups(count, body)

    scale = 1.0 / (rows * cols)
    for p, k in events:
        if p == "compute":
            loaded[k].wait()
            adamw(k, counts[k])
            if not entered:
                pl.semaphore_wait(barrier, len(met))
                entered.append(True)
            for q, piece in enumerate(pieces):
                if piece[1] == k:
                    for m in others(q, 0):
                        reduce_copy(q, 0, m).start()
            continue
        order = orders[pieces[p][3]]
        steps, full = len(order), order[-1][1]
        s = k if k < steps else 2 * steps - 1 - full - k
        arrive(p, s, 0 if k < steps else 1)
        if k + 1 < steps:
            n = size[p, s + 1]
            if not order[s + 1][1]:
                for m in others(p, s + 1):
                    add(p, s, part[p, s + 1, m], n)
                    reduce_copy(p, s + 1, m).start()
                add(p, s, part[p, s + 1, 0], n)
            else:
                add(p, s, part[p, s + 1, 0], n)
                for m in others(p, s + 1):
                    reduce_copy(p, s + 1, m).start()
        else:
            if k + 1 == steps:
                at, n = part[p, s, 0], size[p, s]
                outs[pieces[p][0]][pl.ds(at, n)] = total(p, s, at, n) * scale
            s = 2 * steps - 2 - full - k
            if s >= 0:
                for m in others(p, s):
                    gather_copy(p, s, m).start()
    pltpu.make_async_copy(sent, sent, send_sem.at[0]).wait()


def store(a, b, c, out_a, out_b, out_c, sem):
    copies = [
        pltpu.make_async_copy(src, dst, sem.at[i])
        for i, (src, dst) in enumerate(((a, out_a), (b, out_b), (c, out_c)))
    ]
    for copy in copies:
        copy.start()
    for copy in copies:
        copy.wait()


def as_tiles(x):
    r, c = x.shape
    return x.reshape(r // 8, 8, c // 128, 128).transpose(0, 2, 1, 3).reshape(r * c // 1024, 8, 128)


def from_tiles(x, shape):
    r, c = shape
    return x.reshape(r // 8, c // 128, 8, 128).transpose(0, 2, 1, 3).reshape(r, c)


def solution(mesh):
    rows, cols = mesh.shape["row"], mesh.shape["col"]

    def on_device(*arrays):
        shape = arrays[0].shape[2:]
        tiles = shape[0] * shape[1] // 1024
        orders = stage_orders(rows, cols)
        pieces, events = plan(tiles, orders, rows * cols)
        index, slots = receivers(pieces, events, orders)
        moved = 0
        for _, _, n, name in pieces:
            for bits, full in orders[name]:
                n = n if full else n >> len(bits)
                moved += (1 if full else 2) * ((1 << len(bits)) - 1) * n
        most = max([len(st[0]) for piece in pieces for st in orders[piece[3]] if st[1]], default=1)
        spans = len({piece[1] for piece in pieces})
        result = pl.pallas_call(
            functools.partial(kernel, rows, cols, orders, pieces, events, index),
            out_shape=(pltpu.VMEM((tiles, 8, 128), jnp.float32),) * 3,
            in_specs=[pl.BlockSpec(memory_space=pltpu.HBM)] * 4,
            out_specs=(pl.BlockSpec(memory_space=pltpu.VMEM),) * 3,
            scratch_shapes=[
                pltpu.VMEM((4, tiles, 8, 128), jnp.float32),
                pltpu.VMEM((3, tiles, 8, 128), jnp.float32),
                pltpu.VMEM((3, tiles, 8, 128), jnp.float32),
                pltpu.VMEM(((1 << most) - 1, 3, tiles, 8, 128), jnp.float32),
                pltpu.VMEM((moved, 8, 128), jnp.float32),
                pltpu.SemaphoreType.DMA((spans,)),
                pltpu.SemaphoreType.DMA((1,)),
                pltpu.SemaphoreType.DMA((slots,)),
            ],
            compiler_params=pltpu.CompilerParams(
                collective_id=0, has_side_effects=True, vmem_limit_bytes=48 * 1024 * 1024
            ),
        )(*(pltpu.with_memory_space_constraint(as_tiles(x[0, 0]), pltpu.HBM) for x in arrays))
        result = pl.pallas_call(
            store,
            out_shape=(jax.ShapeDtypeStruct((tiles, 8, 128), jnp.float32),) * 3,
            in_specs=[pl.BlockSpec(memory_space=pltpu.VMEM)] * 3,
            out_specs=(pl.BlockSpec(memory_space=pltpu.HBM),) * 3,
            scratch_shapes=[pltpu.SemaphoreType.DMA((3,))],
        )(*(pltpu.with_memory_space_constraint(x, pltpu.VMEM) for x in result))
        return tuple(from_tiles(x, shape) for x in result)

    in_specs = (P("row", "col", None, None),) * 4
    return jax.shard_map(
        on_device, mesh=mesh, in_specs=in_specs, out_specs=(P(), P(), P()), check_vma=False
    )
```

```python
import functools

import jax
import jax.numpy as jnp
from jax import lax
from jax.experimental import pallas as pl
from jax.experimental.pallas import tpu as pltpu
from jax.sharding import PartitionSpec as P

bias_one = 0.9999734386011124
bias_two = 0.994079470779666
MESH = pl.DeviceIdType.MESH
GROUP = 16


COARSE = 1
COMPUTE_AT = (0, 10, 2, 1, 5, 6, 3, 8)
PIECES = (
    ("d", (4, 24, 62, 86, 114, 143)),
    ("gF", (7, 21, 39, 61, 80, 104, 121)),
    ("d", (11, 25, 42, 70, 90, 107)),
    ("d", (51, 76, 96, 136, 161, 169)),
    ("A2", (40, 63, 83, 111, 132, 150, 162)),
    ("d", (34, 54, 88, 124, 155, 168)),
    ("gF", (14, 28, 46, 75, 101, 125, 139)),
    ("gF", (17, 32, 49, 69, 87, 113, 135)),
    ("A1", (45, 67, 89, 112, 129, 152, 166)),
    ("ux", (12, 29, 48, 68, 91, 108, 127, 149, 160)),
    ("gF", (27, 58, 77, 97, 123, 142, 163)),
    ("d", (9, 26, 53, 73, 98, 119)),
    ("A2", (35, 55, 79, 102, 126, 148, 159)),
    ("A2", (16, 31, 52, 72, 103, 130, 146)),
    ("d", (18, 36, 57, 82, 100, 106)),
    ("gF", (22, 47, 74, 94, 116, 138, 157)),
    ("A1", (37, 59, 85, 109, 128, 141, 153)),
    ("gF", (30, 60, 81, 105, 131, 154, 165)),
    ("d", (13, 33, 56, 92, 115, 133)),
    ("gF", (38, 64, 84, 110, 134, 158, 167)),
    ("d", (20, 41, 78, 117, 151, 164)),
    ("gF", (19, 44, 66, 99, 122, 140, 145)),
    ("A1", (15, 43, 65, 93, 118, 147, 156)),
    ("A2", (23, 50, 71, 95, 120, 137, 144)),
)

def stage_orders(rows, cols):
    row_bits = [("row", b) for b in range((rows - 1).bit_length())]
    col_bits = [("col", b) for b in range((cols - 1).bit_length())]
    core, ys, xs, zs = col_bits[0], col_bits[1:], row_bits[0], row_bits[1:]
    near, far = zs[0], tuple(zs[1:])
    single = lambda bits: [((bit,), False) for bit in bits]
    first = ((core,), False)
    return {
        "x4": [first, ((xs,), False), *single(ys), (tuple(zs), False)],
        "y4": [first, *single(ys), ((xs,), False), (tuple(zs), False)],
        "h": [first, *single(zs), ((xs, *ys), False)],
        "A1": [first, ((xs,), False), ((*ys, near), False), (far, True)],
        "A2": [first, *single(ys), ((xs, near), False), (far, True)],
        "gF": [first, ((near,), False), ((xs, *ys), False), (far, True)],
        "x1": [first, ((xs,), False), *single(ys), ((near,), False), (far, True)],
        "y1": [first, *single(ys), ((xs,), False), ((near,), False), (far, True)],
        "x2": [first, ((xs,), False), ((near,), False), *single(ys), (far, True)],
        "y2": [first, *single(ys), ((near,), False), ((xs,), False), (far, True)],
        "ux": [first, ((near,), False), ((xs,), False), *single(ys), (far, True)],
        "uy": [first, ((near,), False), *single(ys), ((xs,), False), (far, True)],
        "c": [first, ((xs, *ys, near), False), (far, True)],
        "d": [first, ((xs, *ys), False), (tuple(zs), False)],
        "dR": [first, ((xs, *ys), False), ((near,), True), (far, True)],
        "dA": [first, ((xs, *ys), False), (tuple(zs), True)],
    }


def flips(stage, m):
    return tuple(bit for j, bit in enumerate(stage[0]) if m >> j & 1)


def rounds(order):
    return 2 * len(order) - (1 if order[-1][1] else 0)


def plan(tiles, orders, devices):
    pieces, keyed = [], []
    shared = min(len(order[-1][0]) if order[-1][1] else 0 for order in (orders[name] for name, _ in PIECES))
    count = COARSE * devices >> shared
    for i, first in enumerate(range(0, tiles, count)):
        at = COMPUTE_AT[i % len(COMPUTE_AT)]
        keyed.append((at, -1, "compute", first))
        for array in range(3):
            name, keys = PIECES[len(pieces) % len(PIECES)]
            for k in range(rounds(orders[name])):
                extra = max(0, k + 1 - len(keys))
                at = max(at, keys[min(k, len(keys) - 1)] + extra)
                keyed.append((at, len(pieces), k, len(pieces)))
            at = COMPUTE_AT[i % len(COMPUTE_AT)]
            pieces.append((array, first, count, name))
    keyed.sort(key=lambda entry: entry[:2] + (0 if entry[2] == "compute" else entry[2],))
    events = [("compute", at) if k == "compute" else (at, k) for _, _, k, at in keyed]
    return pieces, events


def receivers(pieces, events, orders):
    at = {event: i for i, event in enumerate(events)}
    exchanges = []
    for p, (_, first, _, name) in enumerate(pieces):
        order = orders[name]
        last = rounds(order)
        for s, stage in enumerate(order):
            met = [flips(stage, m) for m in range(1, 1 << len(stage[0]))]
            sent = at["compute", first] if s == 0 else at[p, s - 1]
            exchanges.append((sent, at[p, s], p, s, 0, met))
            if not stage[1]:
                exchanges.append((at[p, last - 2 - s], at[p, last - 1 - s], p, s, 1, met))
    heard = {}
    for sent, waited, _, _, _, met in exchanges:
        for bits in met:
            row = heard.setdefault(bits, [len(events)] * (len(events) + 1))
            row[sent] = min(row[sent], waited)
    for row in heard.values():
        for i in reversed(range(len(events))):
            row[i] = min(row[i], row[i + 1])
    index, ends = {}, []
    for sent, waited, p, s, gather, met in sorted(exchanges, key=lambda e: e[:5]):
        free = [
            (end, j) for j, end in enumerate(ends) if all(heard[bits][end] <= sent for bits in met)
        ]
        j = max(free)[1] if free else len(ends)
        ends[j:j + 1] = [waited]
        index[p, s, gather] = j
    return index, len(ends)


def for_groups(count, body):
    if count <= GROUP:
        body(0, count)
    else:
        def step(i, carry):
            body(i * GROUP, GROUP)
            return carry

        lax.fori_loop(0, count // GROUP, step, 0)


def kernel(rows, cols, orders, pieces, events, index, w_hbm, f_hbm, s_hbm, g_hbm, ow, of, os, ins, acc, got, wide, sent, in_sem, send_sem, recv_sem):
    me = {"row": lax.axis_index("row"), "col": lax.axis_index("col")}
    outs = (ow, of, os)
    every_bit = sorted({bit for stage in orders["x4"] for bit in stage[0]})
    value = {bit: lax.rem(me[bit[0]] // (2 ** bit[1]), 2) for bit in every_bit}

    def peer(bits):
        other = dict(me)
        for bit in bits:
            other[bit[0]] = other[bit[0]] + (1 - 2 * value[bit]) * (2 ** bit[1])
        return other["row"], other["col"]

    spans = sorted({(first, count) for _, first, count, _ in pieces})
    counts = dict(spans)
    loaded = {}
    for i, (first, count) in enumerate(spans):
        for k, src in enumerate((w_hbm, f_hbm, s_hbm, g_hbm)):
            pltpu.make_async_copy(
                src.at[pl.ds(first, count)], ins.at[k, pl.ds(first, count)], in_sem.at[i]
            ).start()
        here = ins.at[:, pl.ds(first, count)]
        loaded[first] = pltpu.make_async_copy(here, here, in_sem.at[i])

    used = {piece[3] for piece in pieces}
    met = sorted({flips(st, m) for o in used for st in orders[o] for m in range(1, 1 << len(st[0]))})
    barrier = pltpu.get_barrier_semaphore()
    for bits in met:
        pl.semaphore_signal(barrier, inc=1, device_id=peer(bits), device_id_type=MESH)
    entered = []

    part, size = {}, {}
    for p, (array, first, count, order) in enumerate(pieces):
        off, n = first, count
        for s, (bits, full) in enumerate(orders[order]):
            n = n if full else n >> len(bits)
            size[p, s] = n
            for m in range(1 << len(bits)):
                at = off
                for j, bit in enumerate(() if full else bits):
                    v = value[bit]
                    at = at + (1 - v if m >> j & 1 else v) * (n << j)
                part[p, s, m] = at
            off = part[p, s, 0]

    def reduce_copy(p, s, m):
        array, n = pieces[p][0], size[p, s]
        land = wide.at[m - 1] if orders[pieces[p][3]][s][1] else got
        return pltpu.make_async_remote_copy(
            src_ref=acc.at[array, pl.ds(part[p, s, m], n)],
            dst_ref=land.at[array, pl.ds(part[p, s, 0], n)],
            send_sem=send_sem.at[0],
            recv_sem=recv_sem.at[index[p, s, 0]],
            device_id=peer(flips(orders[pieces[p][3]][s], m)),
            device_id_type=MESH,
        )

    def gather_copy(p, s, m):
        here = outs[pieces[p][0]].at[pl.ds(part[p, s, 0], size[p, s])]
        return pltpu.make_async_remote_copy(
            src_ref=here,
            dst_ref=here,
            send_sem=send_sem.at[0],
            recv_sem=recv_sem.at[index[p, s, 1]],
            device_id=peer(flips(orders[pieces[p][3]][s], m)),
            device_id_type=MESH,
        )

    def others(p, s):
        return range((1 << len(orders[pieces[p][3]][s][0])) - 1, 0, -1)

    def arrive(p, s, gather):
        array, first = pieces[p][:2]
        here = got.at[array, pl.ds(first, len(others(p, s)) * size[p, s])]
        pltpu.make_async_copy(here, here, recv_sem.at[index[p, s, gather]]).wait()

    def total(p, s, at, n):
        array = pieces[p][0]
        shift = at - part[p, s, 0]
        value = acc[array, pl.ds(at, n)]
        for m in others(p, s):
            land = wide.at[m - 1] if orders[pieces[p][3]][s][1] else got
            value = value + land[array, pl.ds(part[p, s, m] + shift, n)]
        return value

    def add(p, s, at, n):
        def body(i, m):
            acc[pieces[p][0], pl.ds(at + i, m)] = total(p, s, at + i, m)

        for_groups(n, body)

    def adamw(first, count):
        def body(i, m):
            here = pl.ds(first + i, m)
            old, grad = ins[0, here], ins[3, here]
            new_first = 0.9 * ins[1, here] + 0.1 * grad
            new_second = 0.95 * ins[2, here] + 0.05 * grad * grad
            update = (new_first * (1.0 / bias_one)) / (
                jnp.sqrt(new_second * (1.0 / bias_two)) + 1e-08
            ) + 0.1 * old
            acc[0, here] = old - 0.003 * update
            acc[1, here] = new_first
            acc[2, here] = new_second

        for_groups(count, body)

    scale = 1.0 / (rows * cols)
    for p, k in events:
        if p == "compute":
            loaded[k].wait()
            adamw(k, counts[k])
            if not entered:
                pl.semaphore_wait(barrier, len(met))
                entered.append(True)
            for q, piece in enumerate(pieces):
                if piece[1] == k:
                    for m in others(q, 0):
                        reduce_copy(q, 0, m).start()
            continue
        order = orders[pieces[p][3]]
        steps, full = len(order), order[-1][1]
        s = k if k < steps else 2 * steps - 1 - full - k
        arrive(p, s, 0 if k < steps else 1)
        if k + 1 < steps:
            n = size[p, s + 1]
            if not order[s + 1][1]:
                for m in others(p, s + 1):
                    add(p, s, part[p, s + 1, m], n)
                    reduce_copy(p, s + 1, m).start()
                add(p, s, part[p, s + 1, 0], n)
            else:
                add(p, s, part[p, s + 1, 0], n)
                for m in others(p, s + 1):
                    reduce_copy(p, s + 1, m).start()
        else:
            if k + 1 == steps:
                at, n = part[p, s, 0], size[p, s]
                outs[pieces[p][0]][pl.ds(at, n)] = total(p, s, at, n) * scale
            s = 2 * steps - 2 - full - k
            if s >= 0:
                for m in others(p, s):
                    gather_copy(p, s, m).start()
    pltpu.make_async_copy(sent, sent, send_sem.at[0]).wait()


def store(a, b, c, out_a, out_b, out_c, sem):
    copies = [
        pltpu.make_async_copy(src, dst, sem.at[i])
        for i, (src, dst) in enumerate(((a, out_a), (b, out_b), (c, out_c)))
    ]
    for copy in copies:
        copy.start()
    for copy in copies:
        copy.wait()


def as_tiles(x):
    r, c = x.shape
    return x.reshape(r // 8, 8, c // 128, 128).transpose(0, 2, 1, 3).reshape(r * c // 1024, 8, 128)


def from_tiles(x, shape):
    r, c = shape
    return x.reshape(r // 8, c // 128, 8, 128).transpose(0, 2, 1, 3).reshape(r, c)


def solution(mesh):
    rows, cols = mesh.shape["row"], mesh.shape["col"]

    def on_device(*arrays):
        shape = arrays[0].shape[2:]
        tiles = shape[0] * shape[1] // 1024
        orders = stage_orders(rows, cols)
        pieces, events = plan(tiles, orders, rows * cols)
        index, slots = receivers(pieces, events, orders)
        moved = 0
        for _, _, n, name in pieces:
            for bits, full in orders[name]:
                n = n if full else n >> len(bits)
                moved += (1 if full else 2) * ((1 << len(bits)) - 1) * n
        most = max([len(st[0]) for piece in pieces for st in orders[piece[3]] if st[1]], default=1)
        spans = len({piece[1] for piece in pieces})
        result = pl.pallas_call(
            functools.partial(kernel, rows, cols, orders, pieces, events, index),
            out_shape=(pltpu.VMEM((tiles, 8, 128), jnp.float32),) * 3,
            in_specs=[pl.BlockSpec(memory_space=pltpu.HBM)] * 4,
            out_specs=(pl.BlockSpec(memory_space=pltpu.VMEM),) * 3,
            scratch_shapes=[
                pltpu.VMEM((4, tiles, 8, 128), jnp.float32),
                pltpu.VMEM((3, tiles, 8, 128), jnp.float32),
                pltpu.VMEM((3, tiles, 8, 128), jnp.float32),
                pltpu.VMEM(((1 << most) - 1, 3, tiles, 8, 128), jnp.float32),
                pltpu.VMEM((moved, 8, 128), jnp.float32),
                pltpu.SemaphoreType.DMA((spans,)),
                pltpu.SemaphoreType.DMA((1,)),
                pltpu.SemaphoreType.DMA((slots,)),
            ],
            compiler_params=pltpu.CompilerParams(
                collective_id=0, has_side_effects=True, vmem_limit_bytes=48 * 1024 * 1024
            ),
        )(*(pltpu.with_memory_space_constraint(as_tiles(x[0, 0]), pltpu.HBM) for x in arrays))
        result = pl.pallas_call(
            store,
            out_shape=(jax.ShapeDtypeStruct((tiles, 8, 128), jnp.float32),) * 3,
            in_specs=[pl.BlockSpec(memory_space=pltpu.VMEM)] * 3,
            out_specs=(pl.BlockSpec(memory_space=pltpu.HBM),) * 3,
            scratch_shapes=[pltpu.SemaphoreType.DMA((3,))],
        )(*(pltpu.with_memory_space_constraint(x, pltpu.VMEM) for x in result))
        return tuple(from_tiles(x, shape) for x in result)

    in_specs = (P("row", "col", None, None),) * 4
    return jax.shard_map(
        on_device, mesh=mesh, in_specs=in_specs, out_specs=(P(), P(), P()), check_vma=False
    )
```

```python
import functools

import jax
import jax.numpy as jnp
from jax import lax
from jax.experimental import pallas as pl
from jax.experimental.pallas import tpu as pltpu
from jax.sharding import PartitionSpec as P

bias_one = 0.9999734386011124
bias_two = 0.994079470779666
MESH = pl.DeviceIdType.MESH
GROUP = 16


COARSE = 1
COMPUTE_AT = (0, 10, 2, 1, 5, 6, 3, 8)
PIECES = (
    ("d", (4, 24, 62, 86, 114, 143)),
    ("gF", (7, 21, 39, 61, 80, 104, 121)),
    ("d", (11, 25, 42, 70, 90, 107)),
    ("d", (51, 76, 96, 136, 161, 169)),
    ("A2", (40, 63, 83, 111, 132, 150, 162)),
    ("d", (34, 54, 88, 124, 155, 168)),
    ("gF", (14, 28, 46, 75, 101, 125, 138)),
    ("gF", (17, 32, 49, 69, 87, 113, 135)),
    ("A1", (45, 67, 89, 112, 129, 152, 166)),
    ("ux", (12, 29, 48, 68, 91, 108, 127, 149, 160)),
    ("gF", (27, 58, 77, 97, 123, 142, 163)),
    ("d", (9, 26, 53, 73, 98, 119)),
    ("A2", (35, 55, 79, 102, 126, 148, 159)),
    ("A2", (16, 31, 52, 72, 103, 130, 146)),
    ("d", (18, 36, 57, 82, 100, 106)),
    ("gF", (22, 47, 74, 94, 116, 139, 157)),
    ("A1", (37, 59, 85, 109, 128, 141, 153)),
    ("gF", (30, 60, 81, 105, 131, 154, 165)),
    ("d", (13, 33, 56, 92, 115, 133)),
    ("gF", (38, 64, 84, 110, 134, 158, 167)),
    ("d", (20, 41, 78, 117, 151, 164)),
    ("gF", (19, 44, 66, 99, 122, 140, 145)),
    ("A1", (15, 43, 65, 93, 118, 147, 156)),
    ("A2", (23, 50, 71, 95, 120, 137, 144)),
)

def stage_orders(rows, cols):
    row_bits = [("row", b) for b in range((rows - 1).bit_length())]
    col_bits = [("col", b) for b in range((cols - 1).bit_length())]
    core, ys, xs, zs = col_bits[0], col_bits[1:], row_bits[0], row_bits[1:]
    near, far = zs[0], tuple(zs[1:])
    single = lambda bits: [((bit,), False) for bit in bits]
    first = ((core,), False)
    return {
        "x4": [first, ((xs,), False), *single(ys), (tuple(zs), False)],
        "y4": [first, *single(ys), ((xs,), False), (tuple(zs), False)],
        "h": [first, *single(zs), ((xs, *ys), False)],
        "A1": [first, ((xs,), False), ((*ys, near), False), (far, True)],
        "A2": [first, *single(ys), ((xs, near), False), (far, True)],
        "gF": [first, ((near,), False), ((xs, *ys), False), (far, True)],
        "x1": [first, ((xs,), False), *single(ys), ((near,), False), (far, True)],
        "y1": [first, *single(ys), ((xs,), False), ((near,), False), (far, True)],
        "x2": [first, ((xs,), False), ((near,), False), *single(ys), (far, True)],
        "y2": [first, *single(ys), ((near,), False), ((xs,), False), (far, True)],
        "ux": [first, ((near,), False), ((xs,), False), *single(ys), (far, True)],
        "uy": [first, ((near,), False), *single(ys), ((xs,), False), (far, True)],
        "c": [first, ((xs, *ys, near), False), (far, True)],
        "d": [first, ((xs, *ys), False), (tuple(zs), False)],
        "dR": [first, ((xs, *ys), False), ((near,), True), (far, True)],
        "dA": [first, ((xs, *ys), False), (tuple(zs), True)],
    }


def twins(rows, cols):
    x, y = ("row", 0), ("col", 1)
    return {x: y, y: x} if (cols - 1).bit_length() == 2 and rows > 1 else {}


def flips(stage, m):
    return tuple(bit for j, bit in enumerate(stage[0]) if m >> j & 1)


def rounds(order):
    return 2 * len(order) - (1 if order[-1][1] else 0)


def plan(tiles, orders, devices):
    pieces, keyed = [], []
    shared = min(len(order[-1][0]) if order[-1][1] else 0 for order in (orders[name] for name, _ in PIECES))
    count = COARSE * devices >> shared
    for i, first in enumerate(range(0, tiles, count)):
        at = COMPUTE_AT[i % len(COMPUTE_AT)]
        keyed.append((at, -1, "compute", first))
        for array in range(3):
            name, keys = PIECES[len(pieces) % len(PIECES)]
            for k in range(rounds(orders[name])):
                extra = max(0, k + 1 - len(keys))
                at = max(at, keys[min(k, len(keys) - 1)] + extra)
                keyed.append((at, len(pieces), k, len(pieces)))
            at = COMPUTE_AT[i % len(COMPUTE_AT)]
            pieces.append((array, first, count, name))
    keyed.sort(key=lambda entry: entry[:2] + (0 if entry[2] == "compute" else entry[2],))
    events = [("compute", at) if k == "compute" else (at, k) for _, _, k, at in keyed]
    return pieces, events


def receivers(pieces, events, orders):
    at = {event: i for i, event in enumerate(events)}
    exchanges = []
    for p, (_, first, _, name) in enumerate(pieces):
        order = orders[name]
        last = rounds(order)
        for s, stage in enumerate(order):
            met = [flips(stage, m) for m in range(1, 1 << len(stage[0]))]
            sent = at["compute", first] if s == 0 else at[p, s - 1]
            exchanges.append((sent, at[p, s], p, s, 0, met))
            if not stage[1]:
                exchanges.append((at[p, last - 2 - s], at[p, last - 1 - s], p, s, 1, met))
    heard = {}
    for sent, waited, _, _, _, met in exchanges:
        for bits in met:
            row = heard.setdefault(bits, [len(events)] * (len(events) + 1))
            row[sent] = min(row[sent], waited)
    for row in heard.values():
        for i in reversed(range(len(events))):
            row[i] = min(row[i], row[i + 1])
    index, ends = {}, []
    for sent, waited, p, s, gather, met in sorted(exchanges, key=lambda e: e[:5]):
        free = [
            (end, j) for j, end in enumerate(ends) if all(heard[bits][end] <= sent for bits in met)
        ]
        j = max(free)[1] if free else len(ends)
        ends[j:j + 1] = [waited]
        index[p, s, gather] = j
    return index, len(ends)


def for_groups(count, body):
    if count <= GROUP:
        body(0, count)
    else:
        def step(i, carry):
            body(i * GROUP, GROUP)
            return carry

        lax.fori_loop(0, count // GROUP, step, 0)


def kernel(rows, cols, orders, pieces, events, index, w_hbm, f_hbm, s_hbm, g_hbm, ow, of, os, ins, acc, got, wide, sent, in_sem, send_sem, recv_sem):
    me = {"row": lax.axis_index("row"), "col": lax.axis_index("col")}
    outs = (ow, of, os)
    every_bit = sorted({bit for stage in orders["x4"] for bit in stage[0]})
    value = {bit: lax.rem(me[bit[0]] // (2 ** bit[1]), 2) for bit in every_bit}

    core, twin = value[orders["x4"][0][0][0]], twins(rows, cols)
    value.update({a: value[a] + core * (value[b] - value[a]) for a, b in twin.items()})

    def peer(bits):
        other = dict(me)
        for bit in bits:
            step = 1 - 2 * value[bit]
            if bit in twin:
                axis, place = twin[bit]
                other[axis] = other[axis] + core * step * (2 ** place)
                step = (1 - core) * step
            other[bit[0]] = other[bit[0]] + step * (2 ** bit[1])
        return other["row"], other["col"]

    spans = sorted({(first, count) for _, first, count, _ in pieces})
    counts = dict(spans)
    loaded = {}
    for i, (first, count) in enumerate(spans):
        for k, src in enumerate((w_hbm, f_hbm, s_hbm, g_hbm)):
            pltpu.make_async_copy(
                src.at[pl.ds(first, count)], ins.at[k, pl.ds(first, count)], in_sem.at[i]
            ).start()
        here = ins.at[:, pl.ds(first, count)]
        loaded[first] = pltpu.make_async_copy(here, here, in_sem.at[i])

    used = {piece[3] for piece in pieces}
    met = sorted({flips(st, m) for o in used for st in orders[o] for m in range(1, 1 << len(st[0]))})
    barrier = pltpu.get_barrier_semaphore()
    for bits in met:
        pl.semaphore_signal(barrier, inc=1, device_id=peer(bits), device_id_type=MESH)
    entered = []

    part, size = {}, {}
    for p, (array, first, count, order) in enumerate(pieces):
        off, n = first, count
        for s, (bits, full) in enumerate(orders[order]):
            n = n if full else n >> len(bits)
            size[p, s] = n
            for m in range(1 << len(bits)):
                at = off
                for j, bit in enumerate(() if full else bits):
                    v = value[bit]
                    at = at + (1 - v if m >> j & 1 else v) * (n << j)
                part[p, s, m] = at
            off = part[p, s, 0]

    def reduce_copy(p, s, m):
        array, n = pieces[p][0], size[p, s]
        land = wide.at[m - 1] if orders[pieces[p][3]][s][1] else got
        return pltpu.make_async_remote_copy(
            src_ref=acc.at[array, pl.ds(part[p, s, m], n)],
            dst_ref=land.at[array, pl.ds(part[p, s, 0], n)],
            send_sem=send_sem.at[0],
            recv_sem=recv_sem.at[index[p, s, 0]],
            device_id=peer(flips(orders[pieces[p][3]][s], m)),
            device_id_type=MESH,
        )

    def gather_copy(p, s, m):
        here = outs[pieces[p][0]].at[pl.ds(part[p, s, 0], size[p, s])]
        return pltpu.make_async_remote_copy(
            src_ref=here,
            dst_ref=here,
            send_sem=send_sem.at[0],
            recv_sem=recv_sem.at[index[p, s, 1]],
            device_id=peer(flips(orders[pieces[p][3]][s], m)),
            device_id_type=MESH,
        )

    def others(p, s):
        return range((1 << len(orders[pieces[p][3]][s][0])) - 1, 0, -1)

    def arrive(p, s, gather):
        array, first = pieces[p][:2]
        here = got.at[array, pl.ds(first, len(others(p, s)) * size[p, s])]
        pltpu.make_async_copy(here, here, recv_sem.at[index[p, s, gather]]).wait()

    def total(p, s, at, n):
        array = pieces[p][0]
        shift = at - part[p, s, 0]
        value = acc[array, pl.ds(at, n)]
        for m in others(p, s):
            land = wide.at[m - 1] if orders[pieces[p][3]][s][1] else got
            value = value + land[array, pl.ds(part[p, s, m] + shift, n)]
        return value

    def add(p, s, at, n):
        def body(i, m):
            acc[pieces[p][0], pl.ds(at + i, m)] = total(p, s, at + i, m)

        for_groups(n, body)

    def adamw(first, count):
        def body(i, m):
            here = pl.ds(first + i, m)
            old, grad = ins[0, here], ins[3, here]
            new_first = 0.9 * ins[1, here] + 0.1 * grad
            new_second = 0.95 * ins[2, here] + 0.05 * grad * grad
            update = (new_first * (1.0 / bias_one)) / (
                jnp.sqrt(new_second * (1.0 / bias_two)) + 1e-08
            ) + 0.1 * old
            acc[0, here] = old - 0.003 * update
            acc[1, here] = new_first
            acc[2, here] = new_second

        for_groups(count, body)

    scale = 1.0 / (rows * cols)
    for p, k in events:
        if p == "compute":
            loaded[k].wait()
            adamw(k, counts[k])
            if not entered:
                pl.semaphore_wait(barrier, len(met))
                entered.append(True)
            for q, piece in enumerate(pieces):
                if piece[1] == k:
                    for m in others(q, 0):
                        reduce_copy(q, 0, m).start()
            continue
        order = orders[pieces[p][3]]
        steps, full = len(order), order[-1][1]
        s = k if k < steps else 2 * steps - 1 - full - k
        arrive(p, s, 0 if k < steps else 1)
        if k + 1 < steps:
            n = size[p, s + 1]
            if not order[s + 1][1]:
                for m in others(p, s + 1):
                    add(p, s, part[p, s + 1, m], n)
                    reduce_copy(p, s + 1, m).start()
                add(p, s, part[p, s + 1, 0], n)
            else:
                add(p, s, part[p, s + 1, 0], n)
                for m in others(p, s + 1):
                    reduce_copy(p, s + 1, m).start()
        else:
            if k + 1 == steps:
                at, n = part[p, s, 0], size[p, s]
                outs[pieces[p][0]][pl.ds(at, n)] = total(p, s, at, n) * scale
            s = 2 * steps - 2 - full - k
            if s >= 0:
                for m in others(p, s):
                    gather_copy(p, s, m).start()
    pltpu.make_async_copy(sent, sent, send_sem.at[0]).wait()


def store(a, b, c, out_a, out_b, out_c, sem):
    copies = [
        pltpu.make_async_copy(src, dst, sem.at[i])
        for i, (src, dst) in enumerate(((a, out_a), (b, out_b), (c, out_c)))
    ]
    for copy in copies:
        copy.start()
    for copy in copies:
        copy.wait()


def as_tiles(x):
    r, c = x.shape
    return x.reshape(r // 8, 8, c // 128, 128).transpose(0, 2, 1, 3).reshape(r * c // 1024, 8, 128)


def from_tiles(x, shape):
    r, c = shape
    return x.reshape(r // 8, c // 128, 8, 128).transpose(0, 2, 1, 3).reshape(r, c)


def solution(mesh):
    rows, cols = mesh.shape["row"], mesh.shape["col"]

    def on_device(*arrays):
        shape = arrays[0].shape[2:]
        tiles = shape[0] * shape[1] // 1024
        orders = stage_orders(rows, cols)
        pieces, events = plan(tiles, orders, rows * cols)
        index, slots = receivers(pieces, events, orders)
        moved = 0
        for _, _, n, name in pieces:
            for bits, full in orders[name]:
                n = n if full else n >> len(bits)
                moved += (1 if full else 2) * ((1 << len(bits)) - 1) * n
        most = max([len(st[0]) for piece in pieces for st in orders[piece[3]] if st[1]], default=1)
        spans = len({piece[1] for piece in pieces})
        result = pl.pallas_call(
            functools.partial(kernel, rows, cols, orders, pieces, events, index),
            out_shape=(pltpu.VMEM((tiles, 8, 128), jnp.float32),) * 3,
            in_specs=[pl.BlockSpec(memory_space=pltpu.HBM)] * 4,
            out_specs=(pl.BlockSpec(memory_space=pltpu.VMEM),) * 3,
            scratch_shapes=[
                pltpu.VMEM((4, tiles, 8, 128), jnp.float32),
                pltpu.VMEM((3, tiles, 8, 128), jnp.float32),
                pltpu.VMEM((3, tiles, 8, 128), jnp.float32),
                pltpu.VMEM(((1 << most) - 1, 3, tiles, 8, 128), jnp.float32),
                pltpu.VMEM((moved, 8, 128), jnp.float32),
                pltpu.SemaphoreType.DMA((spans,)),
                pltpu.SemaphoreType.DMA((1,)),
                pltpu.SemaphoreType.DMA((slots,)),
            ],
            compiler_params=pltpu.CompilerParams(
                collective_id=0, has_side_effects=True, vmem_limit_bytes=48 * 1024 * 1024
            ),
        )(*(pltpu.with_memory_space_constraint(as_tiles(x[0, 0]), pltpu.HBM) for x in arrays))
        result = pl.pallas_call(
            store,
            out_shape=(jax.ShapeDtypeStruct((tiles, 8, 128), jnp.float32),) * 3,
            in_specs=[pl.BlockSpec(memory_space=pltpu.VMEM)] * 3,
            out_specs=(pl.BlockSpec(memory_space=pltpu.HBM),) * 3,
            scratch_shapes=[pltpu.SemaphoreType.DMA((3,))],
        )(*(pltpu.with_memory_space_constraint(x, pltpu.VMEM) for x in result))
        return tuple(from_tiles(x, shape) for x in result)

    in_specs = (P("row", "col", None, None),) * 4
    return jax.shard_map(
        on_device, mesh=mesh, in_specs=in_specs, out_specs=(P(), P(), P()), check_vma=False
    )
```

```python
import functools

import jax
import jax.numpy as jnp
from jax import lax
from jax.experimental import pallas as pl
from jax.experimental.pallas import tpu as pltpu
from jax.sharding import PartitionSpec as P

bias_one = 0.9999734386011124
bias_two = 0.994079470779666
MESH = pl.DeviceIdType.MESH
GROUP = 16


COARSE = 1
COMPUTE_AT = (0, 10, 2, 1, 5, 6, 3, 8)
PIECES = (
    ("d", (4, 24, 62, 86, 114, 143)),
    ("gF", (7, 21, 39, 61, 80, 104, 121)),
    ("d", (11, 25, 42, 70, 90, 107)),
    ("d", (51, 76, 96, 136, 161, 169)),
    ("A2", (40, 63, 83, 111, 132, 150, 162)),
    ("d", (34, 54, 88, 124, 155, 168)),
    ("gF", (14, 28, 46, 75, 101, 125, 138)),
    ("gF", (17, 32, 49, 69, 87, 113, 135)),
    ("A1", (45, 67, 89, 112, 129, 152, 166)),
    ("ux", (12, 29, 48, 68, 91, 108, 127, 149, 160)),
    ("gF", (27, 58, 77, 97, 123, 142, 163)),
    ("d", (9, 26, 53, 73, 98, 119)),
    ("A2", (35, 55, 79, 102, 126, 148, 159)),
    ("A2", (16, 31, 52, 72, 103, 130, 146)),
    ("d", (18, 36, 57, 82, 100, 106)),
    ("gF", (22, 47, 74, 94, 116, 139, 157)),
    ("A1", (37, 59, 85, 109, 128, 141, 153)),
    ("gF", (30, 60, 81, 105, 131, 154, 165)),
    ("d", (13, 33, 56, 92, 115, 133)),
    ("gF", (38, 64, 84, 110, 134, 158, 167)),
    ("d", (20, 41, 78, 117, 151, 164)),
    ("gF", (19, 44, 66, 99, 122, 140, 145)),
    ("A1", (15, 43, 65, 93, 118, 147, 156)),
    ("A2", (23, 50, 71, 95, 120, 137, 144)),
)

def stage_orders(rows, cols):
    row_bits = [("row", b) for b in range((rows - 1).bit_length())]
    col_bits = [("col", b) for b in range((cols - 1).bit_length())]
    core, ys, xs, zs = col_bits[0], col_bits[1:], row_bits[0], row_bits[1:]
    near, far = zs[0], tuple(zs[1:])
    single = lambda bits: [((bit,), False) for bit in bits]
    first = ((core,), False)
    return {
        "x4": [first, ((xs,), False), *single(ys), (tuple(zs), False)],
        "y4": [first, *single(ys), ((xs,), False), (tuple(zs), False)],
        "h": [first, *single(zs), ((xs, *ys), False)],
        "A1": [first, ((xs,), False), ((*ys, near), False), (far, True)],
        "A2": [first, *single(ys), ((xs, near), False), (far, True)],
        "gF": [first, ((near,), False), ((xs, *ys), False), (far, True)],
        "x1": [first, ((xs,), False), *single(ys), ((near,), False), (far, True)],
        "y1": [first, *single(ys), ((xs,), False), ((near,), False), (far, True)],
        "x2": [first, ((xs,), False), ((near,), False), *single(ys), (far, True)],
        "y2": [first, *single(ys), ((near,), False), ((xs,), False), (far, True)],
        "ux": [first, ((near,), False), ((xs,), False), *single(ys), (far, True)],
        "uy": [first, ((near,), False), *single(ys), ((xs,), False), (far, True)],
        "c": [first, ((xs, *ys, near), False), (far, True)],
        "d": [first, ((xs, *ys), False), (tuple(zs), False)],
        "dR": [first, ((xs, *ys), False), ((near,), True), (far, True)],
        "dA": [first, ((xs, *ys), False), (tuple(zs), True)],
    }


def twins(rows, cols):
    x, y = ("row", 0), ("col", 1)
    return {x: y, y: x} if (cols - 1).bit_length() == 2 and rows > 1 else {}


def flips(stage, m):
    return tuple(bit for j, bit in enumerate(stage[0]) if m >> j & 1)


def rounds(order):
    return 2 * len(order) - (1 if order[-1][1] else 0)


def plan(tiles, orders, devices):
    pieces, keyed = [], []
    shared = min(len(order[-1][0]) if order[-1][1] else 0 for order in (orders[name] for name, _ in PIECES))
    count = COARSE * devices >> shared
    for i, first in enumerate(range(0, tiles, count)):
        at = COMPUTE_AT[i % len(COMPUTE_AT)]
        keyed.append((at, -1, "compute", first))
        for array in range(3):
            name, keys = PIECES[len(pieces) % len(PIECES)]
            for k in range(rounds(orders[name])):
                extra = max(0, k + 1 - len(keys))
                at = max(at, keys[min(k, len(keys) - 1)] + extra)
                keyed.append((at, len(pieces), k, len(pieces)))
            at = COMPUTE_AT[i % len(COMPUTE_AT)]
            pieces.append((array, first, count, name))
    keyed.sort(key=lambda entry: entry[:2] + (0 if entry[2] == "compute" else entry[2],))
    events = [("compute", at) if k == "compute" else (at, k) for _, _, k, at in keyed]
    return pieces, events


def receivers(pieces, events, orders):
    at = {event: i for i, event in enumerate(events)}
    exchanges, spans = [], {}
    for p, (_, first, _, name) in enumerate(pieces):
        order = orders[name]
        last = rounds(order)
        for s, stage in enumerate(order):
            met = [flips(stage, m) for m in range(1, 1 << len(stage[0]))]
            if s == 0:
                spans.setdefault(first, []).append((at[p, 0], p, met))
                continue
            exchanges.append((at[p, s - 1], at[p, s], p, s, 0, met))
            if not stage[1]:
                exchanges.append((at[p, last - 2 - s], at[p, last - 1 - s], p, s, 1, met))
    for first, members in spans.items():
        waited, p, met = min(members)
        exchanges.append((at["compute", first], waited, p, 0, 0, met))
    heard = {}
    for sent, waited, _, _, _, met in exchanges:
        for bits in met:
            row = heard.setdefault(bits, [len(events)] * (len(events) + 1))
            row[sent] = min(row[sent], waited)
    for row in heard.values():
        for i in reversed(range(len(events))):
            row[i] = min(row[i], row[i + 1])
    index, ends = {}, []
    for sent, waited, p, s, gather, met in sorted(exchanges, key=lambda e: e[:5]):
        free = [
            (end, j) for j, end in enumerate(ends) if all(heard[bits][end] <= sent for bits in met)
        ]
        j = max(free)[1] if free else len(ends)
        ends[j:j + 1] = [waited]
        index[p, s, gather] = j
    for members in spans.values():
        for _, p, _ in members:
            index[p, 0, 0] = index[min(members)[1], 0, 0]
            index[p, 0, 1] = len(ends)
    return index, len(ends) + 1


def for_groups(count, body):
    if count <= GROUP:
        body(0, count)
    else:
        def step(i, carry):
            body(i * GROUP, GROUP)
            return carry

        lax.fori_loop(0, count // GROUP, step, 0)


def kernel(rows, cols, orders, pieces, events, index, w_hbm, f_hbm, s_hbm, g_hbm, ow, of, os, ins, acc, got, wide, sent, in_sem, send_sem, recv_sem):
    me = {"row": lax.axis_index("row"), "col": lax.axis_index("col")}
    outs = (ow, of, os)
    every_bit = sorted({bit for stage in orders["x4"] for bit in stage[0]})
    value = {bit: lax.rem(me[bit[0]] // (2 ** bit[1]), 2) for bit in every_bit}

    core, twin = value[orders["x4"][0][0][0]], twins(rows, cols)
    value.update({a: value[a] + core * (value[b] - value[a]) for a, b in twin.items()})

    def peer(bits):
        other = dict(me)
        for bit in bits:
            step = 1 - 2 * value[bit]
            if bit in twin:
                axis, place = twin[bit]
                other[axis] = other[axis] + core * step * (2 ** place)
                step = (1 - core) * step
            other[bit[0]] = other[bit[0]] + step * (2 ** bit[1])
        return other["row"], other["col"]

    spans = sorted({(first, count) for _, first, count, _ in pieces})
    counts = dict(spans)
    loaded = {}
    for i, (first, count) in enumerate(spans):
        for k, src in enumerate((w_hbm, f_hbm, s_hbm, g_hbm)):
            pltpu.make_async_copy(
                src.at[pl.ds(first, count)], ins.at[k, pl.ds(first, count)], in_sem.at[i]
            ).start()
        here = ins.at[:, pl.ds(first, count)]
        loaded[first] = pltpu.make_async_copy(here, here, in_sem.at[i])

    used = {piece[3] for piece in pieces}
    met = sorted({flips(st, m) for o in used for st in orders[o] for m in range(1, 1 << len(st[0]))})
    barrier = pltpu.get_barrier_semaphore()
    for bits in met:
        pl.semaphore_signal(barrier, inc=1, device_id=peer(bits), device_id_type=MESH)
    entered = []

    part, size = {}, {}
    for p, (array, first, count, order) in enumerate(pieces):
        off, n = first, count
        for s, (bits, full) in enumerate(orders[order]):
            n = n if full else n >> len(bits)
            size[p, s] = n
            for m in range(1 << len(bits)):
                at = off
                for j, bit in enumerate(() if full else bits):
                    v = value[bit]
                    at = at + (1 - v if m >> j & 1 else v) * (n << j)
                part[p, s, m] = at
            off = part[p, s, 0]

    def reduce_copy(p, s, m):
        array, n = pieces[p][0], size[p, s]
        land = wide.at[m - 1] if orders[pieces[p][3]][s][1] else got
        return pltpu.make_async_remote_copy(
            src_ref=acc.at[array, pl.ds(part[p, s, m], n)],
            dst_ref=land.at[array, pl.ds(part[p, s, 0], n)],
            send_sem=send_sem.at[0],
            recv_sem=recv_sem.at[index[p, s, 0]],
            device_id=peer(flips(orders[pieces[p][3]][s], m)),
            device_id_type=MESH,
        )

    def gather_copy(p, s, m):
        here = outs[pieces[p][0]].at[pl.ds(part[p, s, 0], size[p, s])]
        return pltpu.make_async_remote_copy(
            src_ref=here,
            dst_ref=here,
            send_sem=send_sem.at[0],
            recv_sem=recv_sem.at[index[p, s, 1]],
            device_id=peer(flips(orders[pieces[p][3]][s], m)),
            device_id_type=MESH,
        )

    def others(p, s):
        return range((1 << len(orders[pieces[p][3]][s][0])) - 1, 0, -1)

    arrived = set()

    def arrive(p, s, gather):
        array, first = pieces[p][:2]
        if s == 0:
            if not gather and first not in arrived:
                here = got.at[:, pl.ds(first, size[p, 0])]
                pltpu.make_async_copy(here, here, recv_sem.at[index[p, 0, 0]]).wait()
                arrived.add(first)
            return
        here = got.at[array, pl.ds(first, len(others(p, s)) * size[p, s])]
        pltpu.make_async_copy(here, here, recv_sem.at[index[p, s, gather]]).wait()

    def total(p, s, at, n):
        array = pieces[p][0]
        shift = at - part[p, s, 0]
        value = acc[array, pl.ds(at, n)]
        for m in others(p, s):
            land = wide.at[m - 1] if orders[pieces[p][3]][s][1] else got
            value = value + land[array, pl.ds(part[p, s, m] + shift, n)]
        return value

    def add(p, s, at, n):
        def body(i, m):
            acc[pieces[p][0], pl.ds(at + i, m)] = total(p, s, at + i, m)

        for_groups(n, body)

    def adamw(first, count):
        def body(i, m):
            here = pl.ds(first + i, m)
            old, grad = ins[0, here], ins[3, here]
            new_first = 0.9 * ins[1, here] + 0.1 * grad
            new_second = 0.95 * ins[2, here] + 0.05 * grad * grad
            update = (new_first * (1.0 / bias_one)) / (
                jnp.sqrt(new_second * (1.0 / bias_two)) + 1e-08
            ) + 0.1 * old
            acc[0, here] = old - 0.003 * update
            acc[1, here] = new_first
            acc[2, here] = new_second

        for_groups(count, body)

    scale = 1.0 / (rows * cols)
    for p, k in events:
        if p == "compute":
            loaded[k].wait()
            adamw(k, counts[k])
            if not entered:
                pl.semaphore_wait(barrier, len(met))
                entered.append(True)
            for q, piece in enumerate(pieces):
                if piece[1] == k:
                    for m in others(q, 0):
                        reduce_copy(q, 0, m).start()
            continue
        order = orders[pieces[p][3]]
        steps, full = len(order), order[-1][1]
        s = k if k < steps else 2 * steps - 1 - full - k
        arrive(p, s, 0 if k < steps else 1)
        if k + 1 < steps:
            n = size[p, s + 1]
            if not order[s + 1][1]:
                for m in others(p, s + 1):
                    add(p, s, part[p, s + 1, m], n)
                    reduce_copy(p, s + 1, m).start()
                add(p, s, part[p, s + 1, 0], n)
            else:
                add(p, s, part[p, s + 1, 0], n)
                for m in others(p, s + 1):
                    reduce_copy(p, s + 1, m).start()
        else:
            if k + 1 == steps:
                at, n = part[p, s, 0], size[p, s]
                outs[pieces[p][0]][pl.ds(at, n)] = total(p, s, at, n) * scale
            s = 2 * steps - 2 - full - k
            if s >= 0:
                for m in others(p, s):
                    gather_copy(p, s, m).start()
    half = got.at[:, pl.ds(0, got.shape[1] // 2)]
    pltpu.make_async_copy(half, half, recv_sem.at[index[0, 0, 1]]).wait()
    pltpu.make_async_copy(sent, sent, send_sem.at[0]).wait()


def store(a, b, c, out_a, out_b, out_c, sem):
    copies = [
        pltpu.make_async_copy(src, dst, sem.at[i])
        for i, (src, dst) in enumerate(((a, out_a), (b, out_b), (c, out_c)))
    ]
    for copy in copies:
        copy.start()
    for copy in copies:
        copy.wait()


def as_tiles(x):
    r, c = x.shape
    return x.reshape(r // 8, 8, c // 128, 128).transpose(0, 2, 1, 3).reshape(r * c // 1024, 8, 128)


def from_tiles(x, shape):
    r, c = shape
    return x.reshape(r // 8, c // 128, 8, 128).transpose(0, 2, 1, 3).reshape(r, c)


def solution(mesh):
    rows, cols = mesh.shape["row"], mesh.shape["col"]

    def on_device(*arrays):
        shape = arrays[0].shape[2:]
        tiles = shape[0] * shape[1] // 1024
        orders = stage_orders(rows, cols)
        pieces, events = plan(tiles, orders, rows * cols)
        index, slots = receivers(pieces, events, orders)
        moved = 0
        for _, _, n, name in pieces:
            for bits, full in orders[name]:
                n = n if full else n >> len(bits)
                moved += (1 if full else 2) * ((1 << len(bits)) - 1) * n
        most = max([len(st[0]) for piece in pieces for st in orders[piece[3]] if st[1]], default=1)
        spans = len({piece[1] for piece in pieces})
        result = pl.pallas_call(
            functools.partial(kernel, rows, cols, orders, pieces, events, index),
            out_shape=(pltpu.VMEM((tiles, 8, 128), jnp.float32),) * 3,
            in_specs=[pl.BlockSpec(memory_space=pltpu.HBM)] * 4,
            out_specs=(pl.BlockSpec(memory_space=pltpu.VMEM),) * 3,
            scratch_shapes=[
                pltpu.VMEM((4, tiles, 8, 128), jnp.float32),
                pltpu.VMEM((3, tiles, 8, 128), jnp.float32),
                pltpu.VMEM((3, tiles, 8, 128), jnp.float32),
                pltpu.VMEM(((1 << most) - 1, 3, tiles, 8, 128), jnp.float32),
                pltpu.VMEM((moved, 8, 128), jnp.float32),
                pltpu.SemaphoreType.DMA((spans,)),
                pltpu.SemaphoreType.DMA((1,)),
                pltpu.SemaphoreType.DMA((slots,)),
            ],
            compiler_params=pltpu.CompilerParams(
                collective_id=0, has_side_effects=True, vmem_limit_bytes=48 * 1024 * 1024
            ),
        )(*(pltpu.with_memory_space_constraint(as_tiles(x[0, 0]), pltpu.HBM) for x in arrays))
        result = pl.pallas_call(
            store,
            out_shape=(jax.ShapeDtypeStruct((tiles, 8, 128), jnp.float32),) * 3,
            in_specs=[pl.BlockSpec(memory_space=pltpu.VMEM)] * 3,
            out_specs=(pl.BlockSpec(memory_space=pltpu.HBM),) * 3,
            scratch_shapes=[pltpu.SemaphoreType.DMA((3,))],
        )(*(pltpu.with_memory_space_constraint(x, pltpu.VMEM) for x in result))
        return tuple(from_tiles(x, shape) for x in result)

    in_specs = (P("row", "col", None, None),) * 4
    return jax.shard_map(
        on_device, mesh=mesh, in_specs=in_specs, out_specs=(P(), P(), P()), check_vma=False
    )
```
